32 devices in a mesh: dp: 8 (over z, core), seq: 4 (over y, x).
Axes of the slice: x: 2, y: 2, z: 4, core: 2. Of those that a mesh axis runs over, the one named last changes fastest.
Arguments:
- images_in: bfloat16 [8, 1376, 1024], P('dp', 'seq'), may hold values from -6 to 6
- valid: int32 [8, 1376], P('dp'), may hold values from 0 to 1, as said below
- cotangent: bfloat16 [8, 1376, 1024], P('dp', 'seq'), may hold values from -6 to 6
- qkv_weight: bfloat16 [2, 1024, 3072], P(None, ('dp', 'seq')), may hold values from -0.1875 to 0.1875
- out_weight: bfloat16 [2, 1024, 1024], P(None, ('dp', 'seq')), may hold values from -1 to 1
- fc1_weight: bfloat16 [2, 1024, 4096], P(None, ('dp', 'seq')), may hold values from -0.1875 to 0.1875
- fc2_weight: bfloat16 [2, 4096, 1024], P(None, ('dp', 'seq')), may hold values from -0.09375 to 0.09375
- gains: bfloat16 [2, 2, 1024], P(None, None, ('dp', 'seq')), may hold values from 0.5 to 1.5
- shifts: bfloat16 [2, 4, 1024], P(None, None, ('dp', 'seq')), may hold values from -3 to 3
- layer_scales: bfloat16 [2, 2, 1024], P(None, None, ('dp', 'seq')), may hold values from 0.29882812 to 1.5
- qv_bias: bfloat16 [2, 2048], P(None, ('dp', 'seq')), may hold values from -3 to 3
- fc1_bias: bfloat16 [2, 4096], P(None, ('dp', 'seq')), may hold values from -3 to 3
Outputs:
- images_out: bfloat16 [8, 1376, 1024], P('dp', 'seq')
- images_grad: bfloat16 [8, 1376, 1024], P('dp', 'seq')
- qkv_weight_grad: float32 [2, 1024, 3072], P(None, ('dp', 'seq'))
- out_weight_grad: float32 [2, 1024, 1024], P(None, ('dp', 'seq'))
- fc1_weight_grad: float32 [2, 1024, 4096], P(None, ('dp', 'seq'))
- fc2_weight_grad: float32 [2, 4096, 1024], P(None, ('dp', 'seq'))
- gains_grad: float32 [2, 2, 1024], P(None, None, ('dp', 'seq'))
- shifts_grad: float32 [2, 4, 1024], P(None, None, ('dp', 'seq'))
- layer_scales_grad: float32 [2, 2, 1024], P(None, None, ('dp', 'seq'))
- qv_bias_grad: float32 [2, 2048], P(None, ('dp', 'seq'))
- fc1_bias_grad: float32 [2, 4096], P(None, ('dp', 'seq'))
The draws below stay inside these ranges and needn't reach their ends.
Inputs may be any that keep to these rules, and one draw needn't show every extreme that they name: `valid`: each image's ones form a prefix of 1370 to 1376 positions, the rest are zeros; some image has exactly 1370 ones.
All inputs are finite; a program needn't handle non-finite values.
Results may differ from the reference program's by a relative error of at most 0.012.
Values may be sent and summed in bfloat16 or wider, within the bound.
No kernel may reach another device: no remote copies, remote signals or barrier semaphores. Data moves between devices by JAX's collectives and lax.ppermute only.
A program may use at most 320 MiB of HBM per device.

```python
import math
import jax
import jax.numpy as jnp
from jax import lax

D = 1024
H = 16
HD = 64
FF = 4096
SEQ = 1376
PAD_MOST = 6
LAYERS = 2
IMAGES = 8


def draw_valid(key, part):
    padding = jax.random.randint(key, (IMAGES,), 0, PAD_MOST + 1)
    padding = padding.at[0].set(PAD_MOST)
    lengths = SEQ - padding
    positions = jnp.arange(SEQ)
    return (positions[None, :] < lengths[:, None]).astype(jnp.int32)


def levels(own_key, dims, split, smallest, high):
    factor_of, own = 1.0, jax.random.fold_in(own_key, 6)
    for dim, shards_of in split:
        heights = jnp.exp(jax.random.uniform(jax.random.fold_in(own, dim), (shards_of,), jnp.float32, smallest / len(split), high / len(split)))
        factor_of = factor_of * jnp.repeat(heights, dims[dim] // shards_of).reshape([-1 if axis == dim else 1 for axis in range(len(dims))])
    return factor_of


def scatter_about(rng, extent, deviation, reach, split=(), kind=jnp.bfloat16):
    factor_of = levels(rng, extent, split, -0.22, 0.18) if split else 1.0
    values = jax.random.normal(rng, extent, jnp.float32) * deviation * factor_of
    return jnp.minimum(jnp.maximum(values, -reach), reach).astype(kind)


def setup_inputs(seed: int = 0) -> dict:
    keys = jax.random.split(jax.random.key(seed), 13)
    return {
        "images_in": scatter_about(keys[0], (IMAGES, SEQ, D), 1.0, 6.0, ((0, 8), (1, 4))),
        "valid": draw_valid(jax.random.fold_in(keys[12], 71), 0),
        "cotangent": scatter_about(keys[2], (IMAGES, SEQ, D), 1.0, 6.0, ((0, 8), (1, 4))),
        "qkv_weight": scatter_about(keys[3], (LAYERS, D, 3 * D), D ** -0.5, 0.1875, ((1, 32),)),
        "out_weight": scatter_about(keys[4], (LAYERS, D, D), (D // 32) ** -0.5, 1.0, ((1, 32),)),
        "fc1_weight": scatter_about(keys[5], (LAYERS, D, FF), D ** -0.5, 0.1875, ((1, 32),)),
        "fc2_weight": scatter_about(keys[6], (LAYERS, FF, D), FF ** -0.5, 0.09375, ((1, 32),)),
        "gains": jnp.clip(1.0 + 0.1 * jax.random.normal(keys[7], (LAYERS, 2, D), jnp.float32), 0.5, 1.5).astype(jnp.bfloat16),
        "shifts": scatter_about(keys[8], (LAYERS, 4, D), 0.5, 3.0, ((2, 32),)),
        "layer_scales": jnp.clip(jnp.exp(math.log(1.5) - 1.6133518 * jax.random.uniform(keys[9], (LAYERS, 2, D), jnp.float32) ** levels(keys[9], (LAYERS, 2, D), ((2, 32),), -0.2, 0.2)), 0.29882812, 1.5).astype(jnp.bfloat16),
        "qv_bias": scatter_about(keys[10], (LAYERS, 2 * D), 0.5, 3.0, ((1, 32),)),
        "fc1_bias": scatter_about(keys[11], (LAYERS, FF), 0.5, 3.0, ((1, 32),)),
    }


@jax.custom_vjp
def low(v):
    return lax.optimization_barrier(v.astype(jnp.bfloat16)).astype(jnp.float32)

@jax.custom_vjp
def low_back(v):
    return v

def low_keep(v):
    return (low(v), None)

def low_pass(kept, grad):
    return (grad,)

def back_keep(v):
    return (v, None)

def back_low(kept, grad):
    return (low(grad),)
low.defvjp(low_keep, low_pass)
low_back.defvjp(back_keep, back_low)
highest = lax.Precision.HIGHEST
epsilon = 1e-06
masked_value = -1000000000.0

def norm_rows(values, gain, shift):
    center = values - lax.optimization_barrier(jnp.mean(values, axis=-1, keepdims=True))
    spread = lax.optimization_barrier(jnp.mean(center * center, axis=-1, keepdims=True))
    return center * lax.rsqrt(spread + epsilon) * gain + shift

def attend_image(packed):
    projected, key_valid = packed
    queries = projected[:, 0]
    key_heads = projected[:, 1]
    value_heads = projected[:, 2]
    raw_scores = jnp.einsum('qhd,khd->hqk', queries, key_heads, precision=highest)
    logits = low_back(HD ** (-0.5) * raw_scores)
    masked = jnp.where(key_valid[None, None, :], logits, masked_value)
    attention_weights = low(jax.nn.softmax(masked, axis=-1))
    return jnp.einsum('hqk,khd->qhd', attention_weights, value_heads, precision=highest)

def layer_forward(stream, key_valid, layer_params):
    qkv_matrix, out_matrix, first_matrix, second_matrix, gain_rows, shift_rows, scale_rows, qv_part, first_bias = layer_params
    normed = low(norm_rows(stream, gain_rows[0], shift_rows[0]))
    qkv_bias = jnp.concatenate([qv_part[:D], jnp.zeros((D,), jnp.float32), qv_part[D:]])
    projected = jnp.einsum('bsd,de->bse', normed, qkv_matrix, precision=highest) + qkv_bias
    projected = low(low_back(projected))
    attend_block = jax.checkpoint(attend_image)
    attended = lax.map(attend_block, (projected.reshape(IMAGES, SEQ, 3, H, HD), key_valid))
    attended = low(low_back(attended.reshape(IMAGES, SEQ, D)))
    branch = low_back(jnp.einsum('bsd,de->bse', attended, out_matrix, precision=highest) + shift_rows[2])
    middle = stream + scale_rows[0] * branch
    normed_two = low(norm_rows(middle, gain_rows[1], shift_rows[1]))
    hidden = low_back(jnp.einsum('bsd,df->bsf', normed_two, first_matrix, precision=highest) + first_bias)
    activated = low(jax.nn.gelu(hidden, approximate=False))
    mlp_out = low_back(jnp.einsum('bsf,fd->bsd', activated, second_matrix, precision=highest) + shift_rows[3])
    return middle + scale_rows[1] * mlp_out

def reference(images_in, valid, cotangent, qkv_weight, out_weight, fc1_weight, fc2_weight, gains, shifts, layer_scales, qv_bias, fc1_bias):
    key_valid = valid > 0

    def forward(stream, qkv_all, out_all, first_all, second_all, gain_all, shift_all, scale_all, qv_all, bias_all):
        for layer_index in range(LAYERS):
            layer_params = (qkv_all[layer_index], out_all[layer_index], first_all[layer_index], second_all[layer_index], gain_all[layer_index], shift_all[layer_index], scale_all[layer_index], qv_all[layer_index], bias_all[layer_index])
            stream = layer_forward(stream, key_valid, layer_params)
        return stream
    inputs = (images_in.astype(jnp.float32), qkv_weight.astype(jnp.float32), out_weight.astype(jnp.float32), fc1_weight.astype(jnp.float32), fc2_weight.astype(jnp.float32), gains.astype(jnp.float32), shifts.astype(jnp.float32), layer_scales.astype(jnp.float32), qv_bias.astype(jnp.float32), fc1_bias.astype(jnp.float32))
    result, pullback = jax.vjp(forward, *inputs)
    weighting = cotangent.astype(jnp.float32) * valid.astype(jnp.float32)[:, :, None]
    gradients = pullback(weighting)
    return (result.astype(jnp.bfloat16), gradients[0].astype(jnp.bfloat16), gradients[1], gradients[2], gradients[3], gradients[4], gradients[5], gradients[6], gradients[7], gradients[8], gradients[9])
```

```python
import jax
import jax.numpy as jnp
from jax import lax
from jax.sharding import PartitionSpec as P

HD = 64
LAYERS = 2


epsilon = 1e-06
masked_value = -1000000000.0


def norm_rows(values, gain, shift):
    center = values - jnp.mean(values, axis=-1, keepdims=True)
    spread = jnp.mean(center * center, axis=-1, keepdims=True)
    return center * lax.rsqrt(spread + epsilon) * gain + shift


def gelu_exact(values):
    return jax.nn.gelu(values, approximate=False)


def pack_layer(pieces):
    qkv, out, first, second, gain, shift, scale, qv, bias = pieces
    rows, width = out.shape

    def units(matrix):
        count = matrix.shape[1] // width
        return matrix.reshape(rows, count, width).transpose(1, 0, 2).reshape(-1, width)

    vector = jnp.concatenate([part.reshape(-1) for part in (gain, shift, scale, qv, bias)])
    extra = jnp.zeros((24 * width,), vector.dtype).at[: vector.shape[0]].set(vector).reshape(24, width)
    return jnp.concatenate([units(qkv), out, units(first), second, extra], axis=0)


def fetch_layer(pieces):
    qkv, out, first, second, gain, shift, scale, qv, bias = pieces
    rows, width = out.shape
    packed = pack_layer(pieces)
    gathered = lax.all_gather(packed, ("dp", "seq"), axis=0, tiled=False)
    devices = gathered.shape[0]

    def matrix(start, count):
        block = gathered[:, start : start + count * rows].reshape(devices, count, rows, width)
        return block.transpose(0, 2, 1, 3).reshape(devices * rows, count * width)

    counts = (qkv.shape[1] // width, 1, first.shape[1] // width)
    at = 0
    matrices = []
    for count in counts:
        matrices.append(matrix(at, count))
        at += count * rows
    matrices.append(gathered[:, at : at + second.shape[0]].reshape(-1, width))
    at += second.shape[0]
    flat = gathered[:, at : at + 1].reshape(devices, width)
    vectors = []
    at = 0
    for part in (gain, shift, scale):
        size = part.size
        piece = flat[:, at : at + size].reshape(devices, part.shape[0], part.shape[1])
        vectors.append(piece.transpose(1, 0, 2).reshape(part.shape[0], -1))
        at += size
    for part in (qv, bias):
        vectors.append(flat[:, at : at + part.size].reshape(-1))
        at += part.size
    return tuple(matrices) + tuple(vectors)


def scatter_layer(gradients, devices):
    qkv, out, first, second, gain, shift, scale, qv, bias = gradients
    width = out.shape[1]
    rows = out.shape[0] // devices
    low = jnp.bfloat16

    def units(matrix):
        count = matrix.shape[1] // width
        block = matrix.astype(low).reshape(devices, rows, count, width)
        return block.transpose(0, 2, 1, 3).reshape(devices, count * rows, width)

    vectors = []
    for part in (gain, shift, scale):
        piece = part.reshape(part.shape[0], devices, -1).transpose(1, 0, 2)
        vectors.append(piece.reshape(devices, -1))
    for part in (qv, bias):
        vectors.append(part.reshape(devices, -1))
    vector = jnp.concatenate(vectors, axis=1).astype(low)
    extra = jnp.pad(vector, ((0, 0), (0, 24 * width - vector.shape[1]))).reshape(devices, 24, width)
    packed = jnp.concatenate(
        [units(qkv), units(out), units(first), second.astype(low).reshape(devices, -1, width), extra],
        axis=1,
    )
    total = lax.psum_scatter(
        packed.reshape(-1, width), ("dp", "seq"), scatter_dimension=0, tiled=True
    ).astype(jnp.float32)
    at = 0
    results = []
    for matrix in (qkv, out, first):
        count = matrix.shape[1] // width
        block = total[at : at + count * rows].reshape(count, rows, width)
        results.append(block.transpose(1, 0, 2).reshape(rows, count * width))
        at += count * rows
    results.append(total[at : at + second.shape[0] // devices])
    at += second.shape[0] // devices
    flat = total[at]
    at = 0
    for part in (gain, shift, scale):
        size = part.size // devices
        results.append(flat[at : at + size].reshape(part.shape[0], -1))
        at += size
    for part in (qv, bias):
        size = part.size // devices
        results.append(flat[at : at + size])
        at += size
    return tuple(results)


def split_heads(head_blocks):
    images, length, _, features = head_blocks.shape
    head_count = features // HD
    queries = head_blocks[:, :, 0].reshape(images, length, head_count, HD)
    key_heads = head_blocks[:, :, 1].reshape(images, length, head_count, HD)
    value_heads = head_blocks[:, :, 2].reshape(images, length, head_count, HD)
    return (queries, key_heads, value_heads)


def attention_forward(head_blocks, keep_keys):
    images, length, _, features = head_blocks.shape
    queries, key_heads, value_heads = split_heads(head_blocks)
    factor = HD ** (-0.5)
    block_rows = length // 2
    outputs = []
    log_parts = []
    for block_index in range(2):
        query_rows = queries[:, block_index * block_rows : (block_index + 1) * block_rows]
        logits = factor * jnp.einsum(
            "bqhd,bkhd->bhqk", query_rows, key_heads, preferred_element_type=jnp.float32
        )
        masked = jnp.where(keep_keys[:, None, None, :], logits, masked_value)
        highest = jnp.max(masked, axis=-1, keepdims=True)
        scaled = jnp.exp(masked - highest)
        totals = jnp.sum(scaled, axis=-1, keepdims=True)
        attention_weights = (scaled / totals).astype(jnp.bfloat16)
        outputs.append(
            jnp.einsum(
                "bhqk,bkhd->bqhd",
                attention_weights,
                value_heads,
                preferred_element_type=jnp.float32,
            )
        )
        log_parts.append(highest + jnp.log(totals))
    attended = (
        jnp.concatenate(outputs, axis=1).astype(jnp.bfloat16).reshape(images, length, features)
    )
    return (attended, jnp.concatenate(log_parts, axis=2))


def attention_backward(head_blocks, log_totals, grad_heads, keep_keys):
    images, length, _, features = head_blocks.shape
    head_count = features // HD
    queries, key_heads, value_heads = split_heads(head_blocks)
    grad_out = grad_heads.reshape(images, length, head_count, HD)
    factor = HD ** (-0.5)
    block_rows = length // 2
    query_grads = []
    key_grad = jnp.zeros((images, length, head_count, HD), jnp.float32)
    value_grad = jnp.zeros((images, length, head_count, HD), jnp.float32)
    for block_index in range(2):
        start = block_index * block_rows
        query_rows = queries[:, start : start + block_rows]
        grad_rows = grad_out[:, start : start + block_rows]
        logits = factor * jnp.einsum(
            "bqhd,bkhd->bhqk", query_rows, key_heads, preferred_element_type=jnp.float32
        )
        masked = jnp.where(keep_keys[:, None, None, :], logits, masked_value)
        probs_block = jnp.exp(masked - log_totals[:, :, start : start + block_rows])
        grad_probs = jnp.einsum(
            "bqhd,bkhd->bhqk", grad_rows, value_heads, preferred_element_type=jnp.float32
        )
        row_dots = jnp.sum(probs_block * grad_probs, axis=-1, keepdims=True)
        grad_logits = (probs_block * (grad_probs - row_dots)).astype(jnp.bfloat16)
        query_grads.append(
            factor
            * jnp.einsum(
                "bhqk,bkhd->bqhd", grad_logits, key_heads, preferred_element_type=jnp.float32
            )
        )
        key_grad = key_grad + factor * jnp.einsum(
            "bhqk,bqhd->bkhd", grad_logits, query_rows, preferred_element_type=jnp.float32
        )
        value_grad = value_grad + jnp.einsum(
            "bhqk,bqhd->bkhd",
            probs_block.astype(jnp.bfloat16),
            grad_rows,
            preferred_element_type=jnp.float32,
        )
    query_grad = jnp.concatenate(query_grads, axis=1)
    stacked = jnp.stack([query_grad, key_grad, value_grad], axis=2)
    return stacked.astype(jnp.bfloat16).reshape(images, length, 3, features)


def forward_layer(stream, keep_keys, gathered):
    (
        qkv_matrix,
        out_matrix,
        first_matrix,
        second_matrix,
        gain_rows,
        shift_rows,
        scale_rows,
        qv_part,
        first_bias,
    ) = gathered
    gain_float = gain_rows.astype(jnp.float32)
    shift_float = shift_rows.astype(jnp.float32)
    scale_float = scale_rows.astype(jnp.float32)
    qv_float = qv_part.astype(jnp.float32)
    images, local_rows, features = stream.shape
    normed = norm_rows(stream, gain_float[0], shift_float[0]).astype(jnp.bfloat16)
    qkv_bias = jnp.concatenate(
        [qv_float[:features], jnp.zeros((features,), jnp.float32), qv_float[features:]]
    )
    projected = (
        jnp.einsum("bsd,de->bse", normed, qkv_matrix, preferred_element_type=jnp.float32) + qkv_bias
    )
    projected = projected.astype(jnp.bfloat16).reshape(images, local_rows, 3, features)
    head_blocks = lax.all_to_all(projected, "seq", split_axis=3, concat_axis=1, tiled=True)
    attended_heads, log_totals = attention_forward(head_blocks, keep_keys)
    attended = lax.all_to_all(attended_heads, "seq", split_axis=1, concat_axis=2, tiled=True)
    branch = (
        jnp.einsum("bsd,de->bse", attended, out_matrix, preferred_element_type=jnp.float32)
        + shift_float[2]
    )
    middle = stream + scale_float[0] * branch
    normed_two = norm_rows(middle, gain_float[1], shift_float[1]).astype(jnp.bfloat16)
    hidden = jnp.einsum(
        "bsd,df->bsf", normed_two, first_matrix, preferred_element_type=jnp.float32
    ) + first_bias.astype(jnp.float32)
    activated = gelu_exact(hidden).astype(jnp.bfloat16)
    mlp_out = (
        jnp.einsum("bsf,fd->bsd", activated, second_matrix, preferred_element_type=jnp.float32)
        + shift_float[3]
    )
    remembered = (
        stream,
        normed,
        head_blocks,
        log_totals,
        attended,
        branch,
        middle,
        normed_two,
        hidden,
        activated,
        mlp_out,
    )
    return (middle + scale_float[1] * mlp_out, remembered)


def backward_layer(upstream, remembered, gathered, keep_keys):
    (
        stream,
        normed,
        head_blocks,
        log_totals,
        attended,
        branch,
        middle,
        normed_two,
        hidden,
        activated,
        mlp_out,
    ) = remembered
    (
        qkv_matrix,
        out_matrix,
        first_matrix,
        second_matrix,
        gain_rows,
        shift_rows,
        scale_rows,
        qv_part,
        first_bias,
    ) = gathered
    gain_float = gain_rows.astype(jnp.float32)
    shift_float = shift_rows.astype(jnp.float32)
    scale_float = scale_rows.astype(jnp.float32)
    images, local_rows, features = upstream.shape
    scale_two_grad = jnp.sum(upstream * mlp_out, axis=(0, 1))
    grad_mlp = (scale_float[1] * upstream).astype(jnp.bfloat16)
    second_matrix_grad = jnp.einsum(
        "bsf,bsd->fd", activated, grad_mlp, preferred_element_type=jnp.float32
    )
    mlp_bias_grad = jnp.sum(grad_mlp.astype(jnp.float32), axis=(0, 1))
    grad_act = jnp.einsum(
        "bsd,fd->bsf", grad_mlp, second_matrix, preferred_element_type=jnp.float32
    )
    _, gelu_pullback = jax.vjp(gelu_exact, hidden)
    grad_hidden = gelu_pullback(grad_act)[0].astype(jnp.bfloat16)
    first_matrix_grad = jnp.einsum(
        "bsd,bsf->df", normed_two, grad_hidden, preferred_element_type=jnp.float32
    )
    first_bias_grad = jnp.sum(grad_hidden.astype(jnp.float32), axis=(0, 1))
    grad_norm_two = jnp.einsum(
        "bsf,df->bsd", grad_hidden, first_matrix, preferred_element_type=jnp.float32
    )
    _, second_norm_pullback = jax.vjp(norm_rows, middle, gain_float[1], shift_float[1])
    grad_middle, second_gain_grad, second_shift_grad = second_norm_pullback(grad_norm_two)
    grad_middle = upstream + grad_middle
    scale_one_grad = jnp.sum(grad_middle * branch, axis=(0, 1))
    grad_branch = (scale_float[0] * grad_middle).astype(jnp.bfloat16)
    out_matrix_grad = jnp.einsum(
        "bsd,bse->de", attended, grad_branch, preferred_element_type=jnp.float32
    )
    branch_bias_grad = jnp.sum(grad_branch.astype(jnp.float32), axis=(0, 1))
    grad_attended = jnp.einsum(
        "bse,de->bsd", grad_branch, out_matrix, preferred_element_type=jnp.float32
    ).astype(jnp.bfloat16)
    grad_heads = lax.all_to_all(grad_attended, "seq", split_axis=2, concat_axis=1, tiled=True)
    grad_blocks = attention_backward(head_blocks, log_totals, grad_heads, keep_keys)
    grad_projected = lax.all_to_all(
        grad_blocks, "seq", split_axis=1, concat_axis=3, tiled=True
    ).reshape(images, local_rows, 3 * features)
    qkv_matrix_grad = jnp.einsum(
        "bsd,bse->de", normed, grad_projected, preferred_element_type=jnp.float32
    )
    column_sums = jnp.sum(grad_projected.astype(jnp.float32), axis=(0, 1))
    qv_bias_grad = jnp.concatenate([column_sums[:features], column_sums[2 * features :]])
    grad_normed = jnp.einsum(
        "bse,de->bsd", grad_projected, qkv_matrix, preferred_element_type=jnp.float32
    )
    _, first_norm_pullback = jax.vjp(norm_rows, stream, gain_float[0], shift_float[0])
    grad_stream, first_gain_grad, first_shift_grad = first_norm_pullback(grad_normed)
    grad_stream = grad_middle + grad_stream
    gradients = (
        qkv_matrix_grad,
        out_matrix_grad,
        first_matrix_grad,
        second_matrix_grad,
        jnp.stack([first_gain_grad, second_gain_grad]),
        jnp.stack([first_shift_grad, second_shift_grad, branch_bias_grad, mlp_bias_grad]),
        jnp.stack([scale_one_grad, scale_two_grad]),
        qv_bias_grad,
        first_bias_grad,
    )
    return (grad_stream, gradients)


def shards(
    images_in,
    valid,
    cotangent,
    qkv_weight,
    out_weight,
    fc1_weight,
    fc2_weight,
    gains,
    shifts,
    layer_scales,
    qv_bias,
    fc1_bias,
):
    parameters = (
        qkv_weight,
        out_weight,
        fc1_weight,
        fc2_weight,
        gains,
        shifts,
        layer_scales,
        qv_bias,
        fc1_bias,
    )
    devices = lax.axis_size(("dp", "seq"))
    keep_keys = valid > 0
    stream = images_in.astype(jnp.float32)
    remembered_layers = []
    fetched_layers = []
    for layer_index in range(LAYERS):
        gathered = fetch_layer(tuple((parameter[layer_index] for parameter in parameters)))
        stream, remembered = forward_layer(stream, keep_keys, gathered)
        remembered_layers.append(remembered)
        fetched_layers.append(gathered)
    images_out = stream.astype(jnp.bfloat16)
    local_rows = images_in.shape[1]
    row_valid = lax.dynamic_slice_in_dim(valid, lax.axis_index("seq") * local_rows, local_rows, 1)
    upstream = cotangent.astype(jnp.float32) * row_valid.astype(jnp.float32)[:, :, None]
    collected = [None] * LAYERS
    for layer_index in range(LAYERS - 1, -1, -1):
        gathered = fetched_layers[layer_index]
        upstream, gradients = backward_layer(
            upstream, remembered_layers[layer_index], gathered, keep_keys
        )
        collected[layer_index] = scatter_layer(gradients, devices)
    stacked = tuple(
        (
            jnp.stack([collected[layer_index][member] for layer_index in range(LAYERS)])
            for member in range(9)
        )
    )
    return (images_out, upstream.astype(jnp.bfloat16)) + tuple(stacked)


def solution(mesh):
    in_specs = (
        P("dp", "seq", None),
        P("dp", None),
        P("dp", "seq", None),
        P(None, ("dp", "seq"), None),
        P(None, ("dp", "seq"), None),
        P(None, ("dp", "seq"), None),
        P(None, ("dp", "seq"), None),
        P(None, None, ("dp", "seq")),
        P(None, None, ("dp", "seq")),
        P(None, None, ("dp", "seq")),
        P(None, ("dp", "seq")),
        P(None, ("dp", "seq")),
    )
    out_specs = (
        P("dp", "seq", None),
        P("dp", "seq", None),
        P(None, ("dp", "seq"), None),
        P(None, ("dp", "seq"), None),
        P(None, ("dp", "seq"), None),
        P(None, ("dp", "seq"), None),
        P(None, None, ("dp", "seq")),
        P(None, None, ("dp", "seq")),
        P(None, None, ("dp", "seq")),
        P(None, ("dp", "seq")),
        P(None, ("dp", "seq")),
    )
    return jax.shard_map(shards, mesh=mesh, in_specs=in_specs, out_specs=out_specs, check_vma=False)
```

```python
import functools
import math

import jax
import jax.numpy as jnp
from jax import lax
from jax.experimental import pallas as pl
from jax.experimental.pallas import tpu as pltpu
from jax.sharding import PartitionSpec as P

HD = 64
LAYERS = 2


epsilon = 1e-06
masked_value = -1000000000.0


def norm_rows(values, gain, shift):
    center = values - jnp.mean(values, axis=-1, keepdims=True)
    spread = jnp.mean(center * center, axis=-1, keepdims=True)
    return center * lax.rsqrt(spread + epsilon) * gain + shift


def gelu_exact(values):
    return jax.nn.gelu(values, approximate=False)


def pack_layer(pieces):
    qkv, out, first, second, gain, shift, scale, qv, bias = pieces
    rows, width = out.shape

    def units(matrix):
        count = matrix.shape[1] // width
        return matrix.reshape(rows, count, width).transpose(1, 0, 2).reshape(-1, width)

    vector = jnp.concatenate([part.reshape(-1) for part in (gain, shift, scale, qv, bias)])
    extra = jnp.zeros((24 * width,), vector.dtype).at[: vector.shape[0]].set(vector).reshape(24, width)
    return jnp.concatenate([units(qkv), out, units(first), second, extra], axis=0)


def fetch_layer(pieces):
    qkv, out, first, second, gain, shift, scale, qv, bias = pieces
    rows, width = out.shape
    packed = pack_layer(pieces)
    gathered = lax.all_gather(packed, ("dp", "seq"), axis=0, tiled=False)
    devices = gathered.shape[0]

    def matrix(start, count):
        block = gathered[:, start : start + count * rows].reshape(devices, count, rows, width)
        return block.transpose(0, 2, 1, 3).reshape(devices * rows, count * width)

    counts = (qkv.shape[1] // width, 1, first.shape[1] // width)
    at = 0
    matrices = []
    for count in counts:
        matrices.append(matrix(at, count))
        at += count * rows
    matrices.append(gathered[:, at : at + second.shape[0]].reshape(-1, width))
    at += second.shape[0]
    flat = gathered[:, at : at + 1].reshape(devices, width)
    vectors = []
    at = 0
    for part in (gain, shift, scale):
        size = part.size
        piece = flat[:, at : at + size].reshape(devices, part.shape[0], part.shape[1])
        vectors.append(piece.transpose(1, 0, 2).reshape(part.shape[0], -1))
        at += size
    for part in (qv, bias):
        vectors.append(flat[:, at : at + part.size].reshape(-1))
        at += part.size
    return tuple(matrices) + tuple(vectors)


def scatter_layer(gradients, devices):
    qkv, out, first, second, gain, shift, scale, qv, bias = gradients
    width = out.shape[1]
    rows = out.shape[0] // devices
    low = jnp.bfloat16

    def units(matrix):
        count = matrix.shape[1] // width
        block = matrix.astype(low).reshape(devices, rows, count, width)
        return block.transpose(0, 2, 1, 3).reshape(devices, count * rows, width)

    vectors = []
    for part in (gain, shift, scale):
        piece = part.reshape(part.shape[0], devices, -1).transpose(1, 0, 2)
        vectors.append(piece.reshape(devices, -1))
    for part in (qv, bias):
        vectors.append(part.reshape(devices, -1))
    vector = jnp.concatenate(vectors, axis=1).astype(low)
    extra = jnp.pad(vector, ((0, 0), (0, 24 * width - vector.shape[1]))).reshape(devices, 24, width)
    packed = jnp.concatenate(
        [units(qkv), units(out), units(first), second.astype(low).reshape(devices, -1, width), extra],
        axis=1,
    )
    total = lax.psum_scatter(
        packed.reshape(-1, width), ("dp", "seq"), scatter_dimension=0, tiled=True
    ).astype(jnp.float32)
    at = 0
    results = []
    for matrix in (qkv, out, first):
        count = matrix.shape[1] // width
        block = total[at : at + count * rows].reshape(count, rows, width)
        results.append(block.transpose(1, 0, 2).reshape(rows, count * width))
        at += count * rows
    results.append(total[at : at + second.shape[0] // devices])
    at += second.shape[0] // devices
    flat = total[at]
    at = 0
    for part in (gain, shift, scale):
        size = part.size // devices
        results.append(flat[at : at + size].reshape(part.shape[0], -1))
        at += size
    for part in (qv, bias):
        size = part.size // devices
        results.append(flat[at : at + size])
        at += size
    return tuple(results)


def split_heads(head_blocks):
    images, length, _, features = head_blocks.shape
    head_count = features // HD
    queries = head_blocks[:, :, 0].reshape(images, length, head_count, HD)
    key_heads = head_blocks[:, :, 1].reshape(images, length, head_count, HD)
    value_heads = head_blocks[:, :, 2].reshape(images, length, head_count, HD)
    return (queries, key_heads, value_heads)


def attention_forward(head_blocks, keep_keys):
    images, length, _, features = head_blocks.shape
    queries, key_heads, value_heads = split_heads(head_blocks)
    factor = HD ** (-0.5)
    block_rows = length // 2
    outputs = []
    log_parts = []
    for block_index in range(2):
        query_rows = queries[:, block_index * block_rows : (block_index + 1) * block_rows]
        logits = factor * jnp.einsum(
            "bqhd,bkhd->bhqk", query_rows, key_heads, preferred_element_type=jnp.float32
        )
        masked = jnp.where(keep_keys[:, None, None, :], logits, masked_value)
        highest = jnp.max(masked, axis=-1, keepdims=True)
        scaled = jnp.exp(masked - highest)
        totals = jnp.sum(scaled, axis=-1, keepdims=True)
        attention_weights = (scaled / totals).astype(jnp.bfloat16)
        outputs.append(
            jnp.einsum(
                "bhqk,bkhd->bqhd",
                attention_weights,
                value_heads,
                preferred_element_type=jnp.float32,
            )
        )
        log_parts.append(highest + jnp.log(totals))
    attended = (
        jnp.concatenate(outputs, axis=1).astype(jnp.bfloat16).reshape(images, length, features)
    )
    return (attended, jnp.concatenate(log_parts, axis=2))


def attention_backward(head_blocks, log_totals, grad_heads, keep_keys):
    images, length, _, features = head_blocks.shape
    head_count = features // HD
    queries, key_heads, value_heads = split_heads(head_blocks)
    grad_out = grad_heads.reshape(images, length, head_count, HD)
    factor = HD ** (-0.5)
    block_rows = length // 2
    query_grads = []
    key_grad = jnp.zeros((images, length, head_count, HD), jnp.float32)
    value_grad = jnp.zeros((images, length, head_count, HD), jnp.float32)
    for block_index in range(2):
        start = block_index * block_rows
        query_rows = queries[:, start : start + block_rows]
        grad_rows = grad_out[:, start : start + block_rows]
        logits = factor * jnp.einsum(
            "bqhd,bkhd->bhqk", query_rows, key_heads, preferred_element_type=jnp.float32
        )
        masked = jnp.where(keep_keys[:, None, None, :], logits, masked_value)
        probs_block = jnp.exp(masked - log_totals[:, :, start : start + block_rows])
        grad_probs = jnp.einsum(
            "bqhd,bkhd->bhqk", grad_rows, value_heads, preferred_element_type=jnp.float32
        )
        row_dots = jnp.sum(probs_block * grad_probs, axis=-1, keepdims=True)
        grad_logits = (probs_block * (grad_probs - row_dots)).astype(jnp.bfloat16)
        query_grads.append(
            factor
            * jnp.einsum(
                "bhqk,bkhd->bqhd", grad_logits, key_heads, preferred_element_type=jnp.float32
            )
        )
        key_grad = key_grad + factor * jnp.einsum(
            "bhqk,bqhd->bkhd", grad_logits, query_rows, preferred_element_type=jnp.float32
        )
        value_grad = value_grad + jnp.einsum(
            "bhqk,bqhd->bkhd",
            probs_block.astype(jnp.bfloat16),
            grad_rows,
            preferred_element_type=jnp.float32,
        )
    query_grad = jnp.concatenate(query_grads, axis=1)
    stacked = jnp.stack([query_grad, key_grad, value_grad], axis=2)
    return stacked.astype(jnp.bfloat16).reshape(images, length, 3, features)


def forward_layer(stream, keep_keys, gathered):
    (
        qkv_matrix,
        out_matrix,
        first_matrix,
        second_matrix,
        gain_rows,
        shift_rows,
        scale_rows,
        qv_part,
        first_bias,
    ) = gathered
    gain_float = gain_rows.astype(jnp.float32)
    shift_float = shift_rows.astype(jnp.float32)
    scale_float = scale_rows.astype(jnp.float32)
    qv_float = qv_part.astype(jnp.float32)
    images, local_rows, features = stream.shape
    normed = norm_rows(stream, gain_float[0], shift_float[0]).astype(jnp.bfloat16)
    qkv_bias = jnp.concatenate(
        [qv_float[:features], jnp.zeros((features,), jnp.float32), qv_float[features:]]
    )
    projected = (
        jnp.einsum("bsd,de->bse", normed, qkv_matrix, preferred_element_type=jnp.float32) + qkv_bias
    )
    projected = projected.astype(jnp.bfloat16).reshape(images, local_rows, 3, features)
    head_blocks = lax.all_to_all(projected, "seq", split_axis=3, concat_axis=1, tiled=True)
    attended_heads, log_totals = attention_forward(head_blocks, keep_keys)
    attended = lax.all_to_all(attended_heads, "seq", split_axis=1, concat_axis=2, tiled=True)
    branch = (
        jnp.einsum("bsd,de->bse", attended, out_matrix, preferred_element_type=jnp.float32)
        + shift_float[2]
    )
    middle = stream + scale_float[0] * branch
    normed_two = norm_rows(middle, gain_float[1], shift_float[1]).astype(jnp.bfloat16)
    hidden = jnp.einsum(
        "bsd,df->bsf", normed_two, first_matrix, preferred_element_type=jnp.float32
    ) + first_bias.astype(jnp.float32)
    activated = gelu_exact(hidden).astype(jnp.bfloat16)
    mlp_out = (
        jnp.einsum("bsf,fd->bsd", activated, second_matrix, preferred_element_type=jnp.float32)
        + shift_float[3]
    )
    remembered = (
        stream,
        normed,
        head_blocks,
        log_totals,
        attended,
        branch,
        middle,
        normed_two,
        hidden,
        activated,
        mlp_out,
    )
    return (middle + scale_float[1] * mlp_out, remembered)


def backward_layer(upstream, remembered, gathered, keep_keys):
    (
        stream,
        normed,
        head_blocks,
        log_totals,
        attended,
        branch,
        middle,
        normed_two,
        hidden,
        activated,
        mlp_out,
    ) = remembered
    (
        qkv_matrix,
        out_matrix,
        first_matrix,
        second_matrix,
        gain_rows,
        shift_rows,
        scale_rows,
        qv_part,
        first_bias,
    ) = gathered
    gain_float = gain_rows.astype(jnp.float32)
    shift_float = shift_rows.astype(jnp.float32)
    scale_float = scale_rows.astype(jnp.float32)
    images, local_rows, features = upstream.shape
    scale_two_grad = jnp.sum(upstream * mlp_out, axis=(0, 1))
    grad_mlp = (scale_float[1] * upstream).astype(jnp.bfloat16)
    second_matrix_grad = jnp.einsum(
        "bsf,bsd->fd", activated, grad_mlp, preferred_element_type=jnp.float32
    )
    mlp_bias_grad = jnp.sum(grad_mlp.astype(jnp.float32), axis=(0, 1))
    grad_act = jnp.einsum(
        "bsd,fd->bsf", grad_mlp, second_matrix, preferred_element_type=jnp.float32
    )
    _, gelu_pullback = jax.vjp(gelu_exact, hidden)
    grad_hidden = gelu_pullback(grad_act)[0].astype(jnp.bfloat16)
    first_matrix_grad = jnp.einsum(
        "bsd,bsf->df", normed_two, grad_hidden, preferred_element_type=jnp.float32
    )
    first_bias_grad = jnp.sum(grad_hidden.astype(jnp.float32), axis=(0, 1))
    grad_norm_two = jnp.einsum(
        "bsf,df->bsd", grad_hidden, first_matrix, preferred_element_type=jnp.float32
    )
    _, second_norm_pullback = jax.vjp(norm_rows, middle, gain_float[1], shift_float[1])
    grad_middle, second_gain_grad, second_shift_grad = second_norm_pullback(grad_norm_two)
    grad_middle = upstream + grad_middle
    scale_one_grad = jnp.sum(grad_middle * branch, axis=(0, 1))
    grad_branch = (scale_float[0] * grad_middle).astype(jnp.bfloat16)
    out_matrix_grad = jnp.einsum(
        "bsd,bse->de", attended, grad_branch, preferred_element_type=jnp.float32
    )
    branch_bias_grad = jnp.sum(grad_branch.astype(jnp.float32), axis=(0, 1))
    grad_attended = jnp.einsum(
        "bse,de->bsd", grad_branch, out_matrix, preferred_element_type=jnp.float32
    ).astype(jnp.bfloat16)
    grad_heads = lax.all_to_all(grad_attended, "seq", split_axis=2, concat_axis=1, tiled=True)
    grad_blocks = attention_backward(head_blocks, log_totals, grad_heads, keep_keys)
    grad_projected = lax.all_to_all(
        grad_blocks, "seq", split_axis=1, concat_axis=3, tiled=True
    ).reshape(images, local_rows, 3 * features)
    qkv_matrix_grad = jnp.einsum(
        "bsd,bse->de", normed, grad_projected, preferred_element_type=jnp.float32
    )
    column_sums = jnp.sum(grad_projected.astype(jnp.float32), axis=(0, 1))
    qv_bias_grad = jnp.concatenate([column_sums[:features], column_sums[2 * features :]])
    grad_normed = jnp.einsum(
        "bse,de->bsd", grad_projected, qkv_matrix, preferred_element_type=jnp.float32
    )
    _, first_norm_pullback = jax.vjp(norm_rows, stream, gain_float[0], shift_float[0])
    grad_stream, first_gain_grad, first_shift_grad = first_norm_pullback(grad_normed)
    grad_stream = grad_middle + grad_stream
    gradients = (
        qkv_matrix_grad,
        out_matrix_grad,
        first_matrix_grad,
        second_matrix_grad,
        jnp.stack([first_gain_grad, second_gain_grad]),
        jnp.stack([first_shift_grad, second_shift_grad, branch_bias_grad, mlp_bias_grad]),
        jnp.stack([scale_one_grad, scale_two_grad]),
        qv_bias_grad,
        first_bias_grad,
    )
    return (grad_stream, gradients)


def shards(
    images_in,
    valid,
    cotangent,
    qkv_weight,
    out_weight,
    fc1_weight,
    fc2_weight,
    gains,
    shifts,
    layer_scales,
    qv_bias,
    fc1_bias,
):
    parameters = (
        qkv_weight,
        out_weight,
        fc1_weight,
        fc2_weight,
        gains,
        shifts,
        layer_scales,
        qv_bias,
        fc1_bias,
    )
    devices = lax.axis_size(("dp", "seq"))
    keep_keys = valid > 0
    stream = images_in.astype(jnp.float32)
    remembered_layers = []
    fetched_layers = []
    for layer_index in range(LAYERS):
        gathered = fetch_layer(tuple((parameter[layer_index] for parameter in parameters)))
        stream, remembered = forward_layer(stream, keep_keys, gathered)
        remembered_layers.append(remembered)
        fetched_layers.append(gathered)
    images_out = stream.astype(jnp.bfloat16)
    local_rows = images_in.shape[1]
    row_valid = lax.dynamic_slice_in_dim(valid, lax.axis_index("seq") * local_rows, local_rows, 1)
    upstream = cotangent.astype(jnp.float32) * row_valid.astype(jnp.float32)[:, :, None]
    collected = [None] * LAYERS
    for layer_index in range(LAYERS - 1, -1, -1):
        gathered = fetched_layers[layer_index]
        upstream, gradients = backward_layer(
            upstream, remembered_layers[layer_index], gathered, keep_keys
        )
        collected[layer_index] = scatter_layer(gradients, devices)
    stacked = tuple(
        (
            jnp.stack([collected[layer_index][member] for layer_index in range(LAYERS)])
            for member in range(9)
        )
    )
    return (images_out, upstream.astype(jnp.bfloat16)) + tuple(stacked)


F32=jnp.float32; BF=jnp.bfloat16
NN=(((1,),(0,)),((),())); NT=(((1,),(1,)),((),())); TN=(((0,),(0,)),((),()))
dd=functools.partial(lax.dot_general,preferred_element_type=F32)
LIMIT=pltpu.CompilerParams(vmem_limit_bytes=60<<20)

def normalize(v):
    c=v-jnp.mean(v,axis=-1,keepdims=True)
    r=lax.rsqrt(jnp.mean(c*c,axis=-1,keepdims=True)+epsilon)
    return c*r,r

def const(*shape): return pl.BlockSpec(shape,lambda *_: (0,)*len(shape))

def qkv_kernel(stream_ref,vec_ref,w_ref,normed_ref,out_ref,*,groups):
    p=pl.program_id(0)
    @pl.when(p==0)
    def _():
        x,_=normalize(stream_ref[...])
        normed_ref[...]=(x*vec_ref[0:1,:]+vec_ref[2:3,:]).astype(BF)
    width=w_ref.shape[-1]
    w=w_ref[...].reshape(-1,width)
    y=dd(normed_ref[...],w,NN)
    b=jnp.where(p==0,vec_ref[8:9,:],jnp.where(p==2,vec_ref[9:10,:],0.0))
    y=(y+b).astype(BF)
    g=width//groups
    for i in range(groups): out_ref[i,0]=y[:,i*g:(i+1)*g]

def qkv_forward(stream,vec,ga,groups):
    T,D=stream.shape
    n,u=ga.shape[:2]
    return pl.pallas_call(functools.partial(qkv_kernel,groups=groups),grid=(3,),
        out_shape=(jax.ShapeDtypeStruct((T,D),BF),jax.ShapeDtypeStruct((groups,3,T,D//groups),BF)),
        in_specs=[const(T,D),const(*vec.shape),pl.BlockSpec((n,4,8,D),lambda p:(0,p,0,0))],
        out_specs=(const(T,D),pl.BlockSpec((groups,1,T,D//groups),lambda p:(0,p,0,0))),
        compiler_params=LIMIT,name="qkv_forward")(stream,vec,ga)

def gelu_pair(v):
    phi=0.5+0.5*lax.erf(v*math.sqrt(0.5))
    return v*phi, phi+v*(jnp.exp(-0.5*v*v)*(1/math.sqrt(2*math.pi)))

def mlp_kernel(att_ref,stream_ref,vec_ref,wo_ref,w1_ref,w2_ref,branch_ref,middle_ref,n2_ref,act_ref,gp_ref,mlp_ref,next_ref,acc):
    f=pl.program_id(0); D=stream_ref.shape[1]
    @pl.when(f==0)
    def _():
        att=jnp.concatenate([att_ref[i] for i in range(att_ref.shape[0])],axis=1)
        branch=dd(att,wo_ref[...].reshape(D,D),NN)+vec_ref[4:5,:]
        branch_ref[...]=branch
        middle=stream_ref[...]+vec_ref[6:7,:]*branch
        middle_ref[...]=middle
        x,_=normalize(middle)
        n2_ref[...]=(x*vec_ref[1:2,:]+vec_ref[3:4,:]).astype(BF)
        acc[...]=jnp.zeros_like(acc)
    hidden=dd(n2_ref[...],w1_ref[...].reshape(D,-1),NN)+vec_ref[pl.ds(10+f,1),:]
    a,gp=gelu_pair(hidden)
    a=a.astype(BF)
    act_ref[...]=a; gp_ref[...]=gp.astype(BF)
    acc[...]+=dd(a,w2_ref[...].reshape(-1,D),NN)
    @pl.when(f==pl.num_programs(0)-1)
    def _():
        m=acc[...]+vec_ref[5:6,:]
        mlp_ref[...]=m
        next_ref[...]=middle_ref[...]+vec_ref[7:8,:]*m

def mlp_forward(att,stream,vec,ga,gb):
    T,D=stream.shape; n=ga.shape[0]
    G=att.shape[0]; nb=4
    S=jax.ShapeDtypeStruct
    return pl.pallas_call(mlp_kernel,grid=(nb,),
        out_shape=(S((T,D),F32),S((T,D),F32),S((T,D),BF),S((T,nb*D),BF),S((T,nb*D),BF),S((T,D),F32),S((T,D),F32)),
        in_specs=[const(*att.shape),const(T,D),const(*vec.shape),
            pl.BlockSpec((n,4,8,D),lambda f:(0,3,0,0)),
            pl.BlockSpec((n,4,8,D),lambda f:(0,f,0,0)),
            pl.BlockSpec((n//nb,16,8,D),lambda f:(f,1,0,0))],
        out_specs=(const(T,D),const(T,D),const(T,D),pl.BlockSpec((T,D),lambda f:(0,f)),pl.BlockSpec((T,D),lambda f:(0,f)),const(T,D),const(T,D)),
        scratch_shapes=[pltpu.VMEM((T,D),F32)],
        compiler_params=LIMIT,name="mlp_forward")(att,stream,vec,ga,gb,gb)

def norm_back(v,u,gain):
    x,r=normalize(v)
    w=u*gain
    dv=r*(w-jnp.mean(w,axis=-1,keepdims=True)-x*jnp.mean(w*x,axis=-1,keepdims=True))
    return dv,jnp.sum(u*x,axis=0,keepdims=True),jnp.sum(u,axis=0,keepdims=True)

def mlp_back_kernel(up_ref,mlp_ref,branch_ref,middle_ref,gp_ref,vec_ref,wo_ref,w1_ref,w2_ref,dall_ref,dmid_ref,datt_ref,sums_ref,acc,dm_s):
    f=pl.program_id(0); D=up_ref.shape[1]
    nb=pl.num_programs(0)-2
    @pl.when(f==0)
    def _():
        u=up_ref[...]
        sums_ref[...]=jnp.zeros_like(sums_ref)
        sums_ref[7:8,:]=jnp.sum(u*mlp_ref[...],axis=0,keepdims=True)
        dm=(vec_ref[7:8,:]*u).astype(BF)
        dm_s[...]=dm
        sums_ref[5:6,:]=jnp.sum(dm.astype(F32),axis=0,keepdims=True)
        acc[...]=jnp.zeros_like(acc)
    @pl.when(f<nb)
    def _():
        da=dd(dm_s[...],w2_ref[...].reshape(-1,D),NT)
        dh=(da*gp_ref[...].astype(F32)).astype(BF)
        dall_ref[...]=dh
        sums_ref[pl.ds(10+f,1),:]=jnp.sum(dh.astype(F32),axis=0,keepdims=True)
        acc[...]+=dd(dh,w1_ref[...].reshape(D,-1),NT)
    @pl.when(f==nb)
    def _():
        dall_ref[...]=dm_s[...]
    @pl.when(f==nb+1)
    def _():
        dv,dg,ds=norm_back(middle_ref[...],acc[...],vec_ref[1:2,:])
        sums_ref[1:2,:]=dg; sums_ref[3:4,:]=ds
        dmid=up_ref[...]+dv
        dmid_ref[...]=dmid
        sums_ref[6:7,:]=jnp.sum(dmid*branch_ref[...],axis=0,keepdims=True)
        db=(vec_ref[6:7,:]*dmid).astype(BF)
        dall_ref[...]=db
        sums_ref[4:5,:]=jnp.sum(db.astype(F32),axis=0,keepdims=True)
        da=dd(db,wo_ref[...].reshape(D,D),NT).astype(BF)
        G=datt_ref.shape[0]; g=D//G
        for i in range(G): datt_ref[i]=da[:,i*g:(i+1)*g]

def mlp_backward(up,mlp,branch,middle,gp,vec,ga,gb,groups):
    T,D=up.shape; n=ga.shape[0]; nb=4
    S=jax.ShapeDtypeStruct
    return pl.pallas_call(mlp_back_kernel,grid=(nb+2,),
        out_shape=(S((T,(nb+2)*D),BF),S((T,D),F32),S((groups,T,D//groups),BF),S((16,D),F32)),
        in_specs=[const(T,D)]*4+[pl.BlockSpec((T,D),lambda f:(0,jnp.minimum(f,nb-1))),const(*vec.shape),
            pl.BlockSpec((n,4,8,D),lambda f:(0,3,0,0)),
            pl.BlockSpec((n,4,8,D),lambda f:(0,jnp.minimum(f,nb-1),0,0)),
            pl.BlockSpec((n//nb,16,8,D),lambda f:(jnp.minimum(f,nb-1),1,0,0))],
        out_specs=(pl.BlockSpec((T,D),lambda f:(0,f)),const(T,D),const(groups,T,D//groups),const(16,D)),
        scratch_shapes=[pltpu.VMEM((T,D),F32),pltpu.VMEM((T,D),BF)],
        compiler_params=LIMIT,name="mlp_backward")(up,mlp,branch,middle,gp,vec,ga,gb,gb)

def qkv_back_kernel(dp_ref,stream_ref,dmid_ref,vec_ref,w_ref,sums_in,up_ref,sums_ref,acc):
    p=pl.program_id(0); D=stream_ref.shape[1]
    G=dp_ref.shape[0]
    @pl.when(p==0)
    def _():
        acc[...]=jnp.zeros_like(acc)
        sums_ref[...]=sums_in[...]
    d=jnp.concatenate([dp_ref[i,0] for i in range(G)],axis=1)
    acc[...]+=dd(d,w_ref[...].reshape(D,D),NT)
    col=jnp.sum(d.astype(F32),axis=0,keepdims=True)
    @pl.when(p==0)
    def _(): sums_ref[8:9,:]=col
    @pl.when(p==2)
    def _():
        sums_ref[9:10,:]=col
        dv,dg,ds=norm_back(stream_ref[...],acc[...],vec_ref[0:1,:])
        sums_ref[0:1,:]=dg; sums_ref[2:3,:]=ds
        up_ref[...]=dmid_ref[...]+dv

def qkv_backward(dp,stream,dmid,vec,ga,sums):
    T,D=stream.shape; n=ga.shape[0]; G=dp.shape[0]
    S=jax.ShapeDtypeStruct
    return pl.pallas_call(qkv_back_kernel,grid=(3,),
        out_shape=(S((T,D),F32),S((16,D),F32)),
        in_specs=[pl.BlockSpec((G,1,T,D//G),lambda p:(0,p,0,0)),const(T,D),const(T,D),const(*vec.shape),
            pl.BlockSpec((n,4,8,D),lambda p:(0,p,0,0)),const(16,D)],
        out_specs=(const(T,D),const(16,D)),
        scratch_shapes=[pltpu.VMEM((T,D),F32)],
        compiler_params=LIMIT,name="qkv_backward")(dp,stream,dmid,vec,ga,sums)


def attn_fwd_kernel(qkv_ref, valid_ref, out_ref, lse_ref, k_s, v_s, *, heads, rows, chunks):
    i=pl.program_id(0)
    width=heads*HD
    keys=rows*chunks
    tail=(keys-6)//128*128
    @pl.when(i==0)
    def _():
        for j in range(chunks):
            k_s[j*rows:(j+1)*rows,:]=qkv_ref[j,1]
            v_s[j*rows:(j+1)*rows,:]=qkv_ref[j,2]
    q=qkv_ref[pl.ds(i,1),0][0]*jnp.bfloat16(HD**-0.5)
    lane=lax.broadcasted_iota(jnp.int32,(1,width),1)//HD
    col=lax.broadcasted_iota(jnp.int32,(1,128),1)
    keep=valid_ref[0:1,tail:keys]>0
    acc=jnp.zeros((rows,width),jnp.float32)
    stats=jnp.zeros((rows,128),jnp.float32)
    for h in range(heads):
        qh=jnp.where(lane==h,q,jnp.zeros_like(q))
        s0=lax.dot_general(qh,k_s[0:tail,:],(((1,),(1,)),((),())),preferred_element_type=jnp.float32)
        s1=lax.dot_general(qh,k_s[tail:keys,:],(((1,),(1,)),((),())),preferred_element_type=jnp.float32)
        s1=jnp.where(keep,s1,masked_value)
        m=jnp.maximum(jnp.max(s0,axis=1,keepdims=True),jnp.max(s1,axis=1,keepdims=True))
        e0=jnp.exp(s0-m); e1=jnp.exp(s1-m)
        t=jnp.sum(e0,axis=1,keepdims=True)+jnp.sum(e1,axis=1,keepdims=True)
        v0=v_s[0:tail,:]; v1=v_s[tail:keys,:]
        o=lax.dot_general(e0.astype(jnp.bfloat16),v0,(((1,),(0,)),((),())),preferred_element_type=jnp.float32)
        o=o+lax.dot_general(e1.astype(jnp.bfloat16),v1,(((1,),(0,)),((),())),preferred_element_type=jnp.float32)
        acc=jnp.where(lane==h,o/t,acc)
        stats=jnp.where(col==h,m+jnp.log(t),stats)
    out_ref[0]=acc.astype(jnp.bfloat16)
    lse_ref[0]=stats.T[0:8,:]

def attn_fwd(qkv,valid):
    chunks,_,rows,width=qkv.shape
    heads=width//HD; keys=rows*chunks
    return pl.pallas_call(
        functools.partial(attn_fwd_kernel,heads=heads,rows=rows,chunks=chunks),
        grid=(chunks,),
        out_shape=(jax.ShapeDtypeStruct((chunks,rows,width),jnp.bfloat16),jax.ShapeDtypeStruct((chunks,8,rows),jnp.float32)),
        in_specs=[pl.BlockSpec((chunks,3,rows,width),lambda i:(0,0,0,0)),pl.BlockSpec((1,keys),lambda i:(0,0))],
        out_specs=(pl.BlockSpec((1,rows,width),lambda i:(i,0,0)),pl.BlockSpec((1,8,rows),lambda i:(i,0,0))),
        scratch_shapes=[pltpu.VMEM((keys,width),jnp.bfloat16)]*2,
        compiler_params=pltpu.CompilerParams(vmem_limit_bytes=60<<20),
        name="attention_forward",
    )(qkv,valid)

def attn_bwd_kernel(qkv_ref, valid_ref, o_ref, g_ref, lse_ref, out_ref, q_s, g_s, dq_s, lse_s, dl_s, *, heads, rows, chunks):
    j=pl.program_id(0)
    width=heads*HD
    keys=rows*chunks
    dd=functools.partial(lax.dot_general,preferred_element_type=jnp.float32)
    lane=lax.broadcasted_iota(jnp.int32,(1,width),1)//HD
    @pl.when(j==0)
    def _():
        hm=(lax.broadcasted_iota(jnp.int32,(8,width),1)//HD==lax.broadcasted_iota(jnp.int32,(8,width),0)).astype(jnp.float32)
        for c in range(chunks):
            sl=slice(c*rows,(c+1)*rows)
            q_s[sl,:]=qkv_ref[c,0]*jnp.bfloat16(HD**-0.5)
            g=g_ref[c]
            g_s[sl,:]=g
            prod=g.astype(jnp.float32)*o_ref[c].astype(jnp.float32)
            dl_s[:,sl]=lax.dot_general(hm,prod,(((1,),(1,)),((),())),precision=lax.Precision.HIGHEST,preferred_element_type=jnp.float32)
            lse_s[:,sl]=lse_ref[c]
        dq_s[...]=jnp.zeros_like(dq_s)
    k=qkv_ref[pl.ds(j,1),1][0]; v=qkv_ref[pl.ds(j,1),2][0]
    keep=valid_ref[0]>0
    dk=jnp.zeros((rows,width),jnp.float32); dv=jnp.zeros((rows,width),jnp.float32)
    q=q_s[...]; g=g_s[...]
    zero=jnp.zeros_like(k)
    for h in range(heads):
        sel=lane==h
        kh=jnp.where(sel,k,zero); vh=jnp.where(sel,v,zero)
        s=dd(kh,q,(((1,),(1,)),((),())))
        s=jnp.where(keep,s,masked_value)
        p=jnp.exp(s-lse_s[h:h+1,:])
        dp=dd(vh,g,(((1,),(1,)),((),())))
        ds=(p*(dp-dl_s[h:h+1,:])).astype(jnp.bfloat16)
        dv=jnp.where(sel,dd(p.astype(jnp.bfloat16),g,(((1,),(0,)),((),()))),dv)
        dk=jnp.where(sel,dd(ds,q,(((1,),(0,)),((),()))),dk)
        dq_s[...]+=dd(ds,kh,(((0,),(0,)),((),())))
    out_ref[pl.ds(j,1),1]=dk.astype(jnp.bfloat16)[None]
    out_ref[pl.ds(j,1),2]=dv.astype(jnp.bfloat16)[None]
    @pl.when(j==chunks-1)
    def _():
        for c in range(chunks):
            out_ref[c,0]=(dq_s[c*rows:(c+1)*rows,:]*HD**-0.5).astype(jnp.bfloat16)

def attn_bwd(qkv,valid_col,o,g,lse):
    chunks,_,rows,width=qkv.shape
    heads=width//HD; keys=rows*chunks
    full=lambda *s: pl.BlockSpec(s,lambda j:(0,)*len(s))
    return pl.pallas_call(
        functools.partial(attn_bwd_kernel,heads=heads,rows=rows,chunks=chunks),
        grid=(chunks,),
        out_shape=jax.ShapeDtypeStruct((chunks,3,rows,width),jnp.bfloat16),
        in_specs=[full(chunks,3,rows,width),pl.BlockSpec((1,rows,1),lambda j:(j,0,0)),full(chunks,rows,width),full(chunks,rows,width),full(chunks,8,rows)],
        out_specs=full(chunks,3,rows,width),
        scratch_shapes=[pltpu.VMEM((keys,width),jnp.bfloat16)]*2+[pltpu.VMEM((keys,width),jnp.float32)]+[pltpu.VMEM((8,keys),jnp.float32)]*2,
        compiler_params=pltpu.CompilerParams(vmem_limit_bytes=60<<20),
        name="attention_backward",
    )(qkv,valid_col,o,g,lse)


def spread(color,idx,unit,src,keep_ref,send_ref,write):
    my,mx=idx[2],idx[3]
    for d in range(2):
        for sent,ref in ((0,keep_ref),(1,send_ref)):
            y=jnp.bitwise_xor(my,d if color==0 else sent)
            x=jnp.bitwise_xor(mx,sent if color==0 else d)
            write(ref,d,y*2+x)

def write_units(color,idx,scr,keep_ref,send_ref):
    def write(ref,d,yx):
        for dz in range(4):
            row=pl.multiple_of(jnp.bitwise_xor(idx[1],dz)*128+yx*32,32)
            ref[d,dz,0]=scr[pl.ds(row,32),:]
    spread(color,idx,32,scr,keep_ref,send_ref,write)

def lhs_columns(idx,ref):
    parts=[]
    for z in range(4):
        at=2*z+idx[0]
        if len(ref.shape)==3:
            per=ref.shape[2]//128
            parts.append(ref[at//per,:,pl.ds(pl.multiple_of((at%per)*128,128),128)])
        else:
            parts.append(ref[:,pl.ds(pl.multiple_of(at*128,128),128)])
    return jnp.concatenate(parts,axis=1)

def pair_product(a,b,x,y):
    return (dd(a,b,TN)+dd(x,y,TN)).astype(BF)

def second_grad_kernel(idx,a_ref,x_ref,b_ref,y_ref,keep_ref,send_ref,scr):
    scr[...]=pair_product(a_ref[...],b_ref[...],x_ref[...],y_ref[...])
    def write(ref,d,yx):
        ref[d,0]=scr[pl.ds(pl.multiple_of(yx*128,128),128),:]
    spread(0,idx,128,scr,keep_ref,send_ref,write)

def second_grad(idx,act,act_o,dall,dall_o):
    T=act.shape[0]; D=1024
    S=jax.ShapeDtypeStruct((2,4,128,D),BF)
    xs=pl.BlockSpec((T,512),lambda s,i:(0,2*s+i[0])); ys=pl.BlockSpec((T,D),lambda s,i:(0,4))
    out=pl.BlockSpec((2,1,128,D),lambda s,i:(0,jnp.bitwise_xor(s,i[1]),0,0))
    return pl.pallas_call(second_grad_kernel,out_shape=(S,S),
        grid_spec=pltpu.PrefetchScalarGridSpec(num_scalar_prefetch=1,grid=(4,),in_specs=[xs,xs,ys,ys],out_specs=(out,out),
            scratch_shapes=[pltpu.VMEM((512,D),BF)]),
        compiler_params=LIMIT,name="second_grad")(idx,act,act_o,dall,dall_o)

def first_grad_kernel(idx,a_ref,x_ref,b_ref,y_ref,keep_ref,send_ref,scr):
    scr[...]=pair_product(lhs_columns(idx,a_ref),b_ref[...],lhs_columns(idx,x_ref),y_ref[...])
    write_units(1,idx,scr,keep_ref,send_ref)

def first_grad(idx,n2,n2_o,dall,dall_o):
    T,D=n2.shape
    S=jax.ShapeDtypeStruct((2,4,4,32,D),BF)
    xs=pl.BlockSpec((T,D),lambda s,i:(0,0)); ys=pl.BlockSpec((T,D),lambda s,i:(0,s))
    out=pl.BlockSpec((2,4,1,32,D),lambda s,i:(0,0,s,0,0))
    return pl.pallas_call(first_grad_kernel,out_shape=(S,S),
        grid_spec=pltpu.PrefetchScalarGridSpec(num_scalar_prefetch=1,grid=(4,),in_specs=[xs,xs,ys,ys],out_specs=(out,out),
            scratch_shapes=[pltpu.VMEM((512,D),BF)]),
        compiler_params=LIMIT,name="first_grad")(idx,n2,n2_o,dall,dall_o)

def attention_grad_kernel(idx,att_ref,att_o,norm_ref,norm_o,db_ref,db_o,dp_ref,dp_o,keep_a,send_a,keep_b,send_b,scr):
    s=pl.program_id(0)
    @pl.when(s==0)
    def _():
        scr[...]=pair_product(lhs_columns(idx,att_ref),db_ref[...],lhs_columns(idx,att_o),db_o[...])
    @pl.when(s>0)
    def _():
        G=dp_ref.shape[0]
        y=jnp.concatenate([dp_ref[i,0] for i in range(G)],axis=1)
        yo=jnp.concatenate([dp_o[i,0] for i in range(G)],axis=1)
        scr[...]=pair_product(lhs_columns(idx,norm_ref),y,lhs_columns(idx,norm_o),yo)
    @pl.when(s<2)
    def _(): write_units(0,idx,scr,keep_a,send_a)
    @pl.when(s>=2)
    def _(): write_units(1,idx,scr,keep_b,send_b)

def attention_grad(idx,att,att_o,normed,normed_o,dall,dall_o,dp,dp_o):
    T,D=normed.shape; G=att.shape[0]
    S=jax.ShapeDtypeStruct((2,4,2,32,D),BF)
    full=lambda a: pl.BlockSpec(a.shape,lambda s,i:(0,)*a.ndim)
    db=pl.BlockSpec((T,D),lambda s,i:(0,5)); dps=pl.BlockSpec((G,1,T,D//G),lambda s,i:(0,jnp.maximum(s-1,0),0,0))
    oa=pl.BlockSpec((2,4,1,32,D),lambda s,i:(0,0,jnp.minimum(s,1),0,0))
    ob=pl.BlockSpec((2,4,1,32,D),lambda s,i:(0,0,jnp.maximum(s-2,0),0,0))
    return pl.pallas_call(attention_grad_kernel,out_shape=(S,S,S,S),
        grid_spec=pltpu.PrefetchScalarGridSpec(num_scalar_prefetch=1,grid=(4,),
            in_specs=[full(att),full(att),full(normed),full(normed),db,db,dps,dps],out_specs=(oa,oa,ob,ob),
            scratch_shapes=[pltpu.VMEM((512,D),BF)]),
        compiler_params=LIMIT,name="attention_grad")(idx,att,att_o,normed,normed_o,dall,dall_o,dp,dp_o)

def is_fast(mesh):
    return mesh.shape["dp"]==8 and mesh.shape["seq"]==4

def swap(v,axis,step):
    return lax.ppermute(v,axis,[(i,i^step) for i in range(lax.axis_size(axis))])

def add(a,b):
    return (a.astype(F32)+b.astype(F32)).astype(BF)

def collect(keep_a,send_a,keep_b,send_b):
    got_a=swap(send_a,"seq",1); got_b=swap(send_b,"seq",2)
    next_a=add(keep_a[1],got_a[1]); stay_a=add(keep_a[0],got_a[0])
    next_b=add(keep_b[1],got_b[1]); stay_b=add(keep_b[0],got_b[0])
    got_a=swap(next_a,"seq",2); got_b=swap(next_b,"seq",1)
    rows=lambda v: v.reshape(4,-1,v.shape[-1])
    whole=jnp.concatenate([rows(add(stay_a,got_a)),rows(add(stay_b,got_b))],axis=1)
    total=whole[0].astype(F32)
    for step in range(1,4):
        total=total+swap(whole[step],"dp",2*step).astype(F32)
    return total

def pack_rows(pieces):
    return jnp.concatenate(pieces,axis=0)

def fast_shards(images_in,valid,cotangent,qkv_weight,out_weight,fc1_weight,fc2_weight,gains,shifts,layer_scales,qv_bias,fc1_bias):
    layers=qkv_weight.shape[0]
    rows,D=out_weight.shape[1:]
    T=images_in.shape[1]
    n=lax.axis_size(("dp","seq")); G=lax.axis_size("seq")
    dp=lax.axis_index("dp"); seq=lax.axis_index("seq")
    idx=jnp.stack([dp%2,dp//2,seq//2,seq%2]).astype(jnp.int32)
    units=lambda m: m.reshape(rows,-1,D).transpose(1,0,2).reshape(-1,D)
    vectors=jnp.concatenate([v.reshape(layers,-1) for v in (gains,shifts,layer_scales,qv_bias,fc1_bias)],axis=1)
    size=vectors.shape[1]
    extra=jnp.zeros((8,D),BF).at[:layers,:size].set(vectors)
    wa=[];wb=[]
    for l in range(layers):
        pa=[units(qkv_weight[l]),out_weight[l]]+([extra] if l==0 else [])
        wa.append(lax.all_gather(pack_rows(pa),("dp","seq"),axis=0,tiled=False))
        wb.append(lax.all_gather(pack_rows([units(fc1_weight[l]),fc2_weight[l]]),("dp","seq"),axis=0,tiled=False))
    flat=wa[0][:,4*rows:4*rows+layers,:size].astype(F32)
    part=8*rows
    first=flat[:,:,:part].reshape(n,layers,8,rows).transpose(1,2,0,3).reshape(layers,8,D)
    second=flat[:,:,part:part+2*rows].transpose(1,0,2).reshape(layers,2,D)
    third=flat[:,:,part+2*rows:].transpose(1,0,2).reshape(layers,4,D)
    vecs=jnp.concatenate([first,second,third,jnp.zeros((layers,2,D),F32)],axis=1)
    wa=[w.reshape(n,-1,8,D) for w in wa]; wb=[w.reshape(n,-1,8,D) for w in wb]
    stream=images_in[0].astype(F32)
    keep=[]
    for l in range(layers):
        normed,proj=qkv_forward(stream,vecs[l],wa[l],G)
        heads=lax.all_to_all(proj,"seq",split_axis=0,concat_axis=0,tiled=True)
        out,lse=attn_fwd(heads,valid)
        att=lax.all_to_all(out,"seq",split_axis=0,concat_axis=0,tiled=True)
        branch,middle,n2,act,gp,mlp,after=mlp_forward(att,stream,vecs[l],wa[l],wb[l])
        others=[swap(v,"dp",1) for v in (normed,att,n2,act)]
        keep.append((stream,normed,heads,out,lse,att,branch,middle,n2,act,gp,mlp,others))
        stream=after
    images_out=stream.astype(BF)[None]
    own=lax.dynamic_slice_in_dim(valid,seq*T,T,1)
    up=cotangent[0].astype(F32)*own.astype(F32).reshape(T,1)
    column=valid.reshape(G,T,1)
    done=[None]*layers; sums_all=[None]*layers
    for l in range(layers-1,-1,-1):
        stream,normed,heads,out,lse,att,branch,middle,n2,act,gp,mlp,(normed_o,att_o,n2_o,act_o)=keep[l]
        dall,dmid,datt,sums=mlp_backward(up,mlp,branch,middle,gp,vecs[l],wa[l],wb[l],G)
        dheads=lax.all_to_all(datt,"seq",split_axis=0,concat_axis=0,tiled=True)
        dall_o=swap(dall,"dp",1)
        keep_a,send_a=second_grad(idx,act,act_o,dall,dall_o)
        keep_b,send_b=first_grad(idx,n2,n2_o,dall,dall_o)
        mlp_total=collect(keep_a,send_a,keep_b,send_b)
        dqkv=attn_bwd(heads,column,out,dheads,lse)
        dproj=lax.all_to_all(dqkv,"seq",split_axis=0,concat_axis=0,tiled=True)
        dproj_o=swap(dproj,"dp",1)
        att_total=collect(*attention_grad(idx,att,att_o,normed,normed_o,dall,dall_o,dproj,dproj_o))
        up,sums_all[l]=qkv_backward(dproj,stream,dmid,vecs[l],wa[l],sums)
        done[l]=(mlp_total,att_total)
    totals=lax.psum(jnp.stack(sums_all),("dp","seq"))
    me=dp*G+seq
    cut=lambda v,width: lax.dynamic_slice_in_dim(v,me*width,width,v.ndim-1)
    small=cut(totals[:,:8],rows)
    qv=cut(totals[:,8:10].reshape(layers,-1),2*rows)
    bias=cut(totals[:,10:14].reshape(layers,-1),4*rows)
    wide=lambda v: v.reshape(-1,rows,D).transpose(1,0,2).reshape(rows,-1)
    join=lambda f: jnp.stack([f(*done[l]) for l in range(layers)])
    gq=join(lambda m,a: wide(a[rows:4*rows]))
    go=join(lambda m,a: a[:rows])
    g1=join(lambda m,a: wide(m[4*rows:8*rows]))
    g2=join(lambda m,a: m[:4*rows])
    return (images_out,up.astype(BF)[None],gq,go,g1,g2,small[:,0:2],small[:,2:6],small[:,6:8],qv,bias)


def solution(mesh):
    in_specs = (
        P("dp", "seq", None),
        P("dp", None),
        P("dp", "seq", None),
        P(None, ("dp", "seq"), None),
        P(None, ("dp", "seq"), None),
        P(None, ("dp", "seq"), None),
        P(None, ("dp", "seq"), None),
        P(None, None, ("dp", "seq")),
        P(None, None, ("dp", "seq")),
        P(None, None, ("dp", "seq")),
        P(None, ("dp", "seq")),
        P(None, ("dp", "seq")),
    )
    out_specs = (
        P("dp", "seq", None),
        P("dp", "seq", None),
        P(None, ("dp", "seq"), None),
        P(None, ("dp", "seq"), None),
        P(None, ("dp", "seq"), None),
        P(None, ("dp", "seq"), None),
        P(None, None, ("dp", "seq")),
        P(None, None, ("dp", "seq")),
        P(None, None, ("dp", "seq")),
        P(None, ("dp", "seq")),
        P(None, ("dp", "seq")),
    )
    return jax.shard_map(fast_shards if is_fast(mesh) else shards, mesh=mesh, in_specs=in_specs, out_specs=out_specs, check_vma=False)
```

```python
import functools
import math

import jax
import jax.numpy as jnp
from jax import lax
from jax.experimental import pallas as pl
from jax.experimental.pallas import tpu as pltpu
from jax.sharding import PartitionSpec as P


HD = 64
LAYERS = 2


epsilon = 1e-06
masked_value = -1000000000.0


def norm_rows(values, gain, shift):
    center = values - jnp.mean(values, axis=-1, keepdims=True)
    spread = jnp.mean(center * center, axis=-1, keepdims=True)
    return center * lax.rsqrt(spread + epsilon) * gain + shift


def gelu_exact(values):
    return jax.nn.gelu(values, approximate=False)


def pack_layer(pieces):
    qkv, out, first, second, gain, shift, scale, qv, bias = pieces
    rows, width = out.shape

    def units(matrix):
        count = matrix.shape[1] // width
        return matrix.reshape(rows, count, width).transpose(1, 0, 2).reshape(-1, width)

    vector = jnp.concatenate([part.reshape(-1) for part in (gain, shift, scale, qv, bias)])
    extra = jnp.zeros((24 * width,), vector.dtype).at[: vector.shape[0]].set(vector).reshape(24, width)
    return jnp.concatenate([units(qkv), out, units(first), second, extra], axis=0)


def fetch_layer(pieces):
    qkv, out, first, second, gain, shift, scale, qv, bias = pieces
    rows, width = out.shape
    packed = pack_layer(pieces)
    gathered = lax.all_gather(packed, ("dp", "seq"), axis=0, tiled=False)
    devices = gathered.shape[0]

    def matrix(start, count):
        block = gathered[:, start : start + count * rows].reshape(devices, count, rows, width)
        return block.transpose(0, 2, 1, 3).reshape(devices * rows, count * width)

    counts = (qkv.shape[1] // width, 1, first.shape[1] // width)
    at = 0
    matrices = []
    for count in counts:
        matrices.append(matrix(at, count))
        at += count * rows
    matrices.append(gathered[:, at : at + second.shape[0]].reshape(-1, width))
    at += second.shape[0]
    flat = gathered[:, at : at + 1].reshape(devices, width)
    vectors = []
    at = 0
    for part in (gain, shift, scale):
        size = part.size
        piece = flat[:, at : at + size].reshape(devices, part.shape[0], part.shape[1])
        vectors.append(piece.transpose(1, 0, 2).reshape(part.shape[0], -1))
        at += size
    for part in (qv, bias):
        vectors.append(flat[:, at : at + part.size].reshape(-1))
        at += part.size
    return tuple(matrices) + tuple(vectors)


def scatter_layer(gradients, devices):
    qkv, out, first, second, gain, shift, scale, qv, bias = gradients
    width = out.shape[1]
    rows = out.shape[0] // devices
    low = jnp.bfloat16

    def units(matrix):
        count = matrix.shape[1] // width
        block = matrix.astype(low).reshape(devices, rows, count, width)
        return block.transpose(0, 2, 1, 3).reshape(devices, count * rows, width)

    vectors = []
    for part in (gain, shift, scale):
        piece = part.reshape(part.shape[0], devices, -1).transpose(1, 0, 2)
        vectors.append(piece.reshape(devices, -1))
    for part in (qv, bias):
        vectors.append(part.reshape(devices, -1))
    vector = jnp.concatenate(vectors, axis=1).astype(low)
    extra = jnp.pad(vector, ((0, 0), (0, 24 * width - vector.shape[1]))).reshape(devices, 24, width)
    packed = jnp.concatenate(
        [units(qkv), units(out), units(first), second.astype(low).reshape(devices, -1, width), extra],
        axis=1,
    )
    total = lax.psum_scatter(
        packed.reshape(-1, width), ("dp", "seq"), scatter_dimension=0, tiled=True
    ).astype(jnp.float32)
    at = 0
    results = []
    for matrix in (qkv, out, first):
        count = matrix.shape[1] // width
        block = total[at : at + count * rows].reshape(count, rows, width)
        results.append(block.transpose(1, 0, 2).reshape(rows, count * width))
        at += count * rows
    results.append(total[at : at + second.shape[0] // devices])
    at += second.shape[0] // devices
    flat = total[at]
    at = 0
    for part in (gain, shift, scale):
        size = part.size // devices
        results.append(flat[at : at + size].reshape(part.shape[0], -1))
        at += size
    for part in (qv, bias):
        size = part.size // devices
        results.append(flat[at : at + size])
        at += size
    return tuple(results)


def split_heads(head_blocks):
    images, length, _, features = head_blocks.shape
    head_count = features // HD
    queries = head_blocks[:, :, 0].reshape(images, length, head_count, HD)
    key_heads = head_blocks[:, :, 1].reshape(images, length, head_count, HD)
    value_heads = head_blocks[:, :, 2].reshape(images, length, head_count, HD)
    return (queries, key_heads, value_heads)


def attention_forward(head_blocks, keep_keys):
    images, length, _, features = head_blocks.shape
    queries, key_heads, value_heads = split_heads(head_blocks)
    factor = HD ** (-0.5)
    block_rows = length // 2
    outputs = []
    log_parts = []
    for block_index in range(2):
        query_rows = queries[:, block_index * block_rows : (block_index + 1) * block_rows]
        logits = factor * jnp.einsum(
            "bqhd,bkhd->bhqk", query_rows, key_heads, preferred_element_type=jnp.float32
        )
        masked = jnp.where(keep_keys[:, None, None, :], logits, masked_value)
        highest = jnp.max(masked, axis=-1, keepdims=True)
        scaled = jnp.exp(masked - highest)
        totals = jnp.sum(scaled, axis=-1, keepdims=True)
        attention_weights = (scaled / totals).astype(jnp.bfloat16)
        outputs.append(
            jnp.einsum(
                "bhqk,bkhd->bqhd",
                attention_weights,
                value_heads,
                preferred_element_type=jnp.float32,
            )
        )
        log_parts.append(highest + jnp.log(totals))
    attended = (
        jnp.concatenate(outputs, axis=1).astype(jnp.bfloat16).reshape(images, length, features)
    )
    return (attended, jnp.concatenate(log_parts, axis=2))


def attention_backward(head_blocks, log_totals, grad_heads, keep_keys):
    images, length, _, features = head_blocks.shape
    head_count = features // HD
    queries, key_heads, value_heads = split_heads(head_blocks)
    grad_out = grad_heads.reshape(images, length, head_count, HD)
    factor = HD ** (-0.5)
    block_rows = length // 2
    query_grads = []
    key_grad = jnp.zeros((images, length, head_count, HD), jnp.float32)
    value_grad = jnp.zeros((images, length, head_count, HD), jnp.float32)
    for block_index in range(2):
        start = block_index * block_rows
        query_rows = queries[:, start : start + block_rows]
        grad_rows = grad_out[:, start : start + block_rows]
        logits = factor * jnp.einsum(
            "bqhd,bkhd->bhqk", query_rows, key_heads, preferred_element_type=jnp.float32
        )
        masked = jnp.where(keep_keys[:, None, None, :], logits, masked_value)
        probs_block = jnp.exp(masked - log_totals[:, :, start : start + block_rows])
        grad_probs = jnp.einsum(
            "bqhd,bkhd->bhqk", grad_rows, value_heads, preferred_element_type=jnp.float32
        )
        row_dots = jnp.sum(probs_block * grad_probs, axis=-1, keepdims=True)
        grad_logits = (probs_block * (grad_probs - row_dots)).astype(jnp.bfloat16)
        query_grads.append(
            factor
            * jnp.einsum(
                "bhqk,bkhd->bqhd", grad_logits, key_heads, preferred_element_type=jnp.float32
            )
        )
        key_grad = key_grad + factor * jnp.einsum(
            "bhqk,bqhd->bkhd", grad_logits, query_rows, preferred_element_type=jnp.float32
        )
        value_grad = value_grad + jnp.einsum(
            "bhqk,bqhd->bkhd",
            probs_block.astype(jnp.bfloat16),
            grad_rows,
            preferred_element_type=jnp.float32,
        )
    query_grad = jnp.concatenate(query_grads, axis=1)
    stacked = jnp.stack([query_grad, key_grad, value_grad], axis=2)
    return stacked.astype(jnp.bfloat16).reshape(images, length, 3, features)


def forward_layer(stream, keep_keys, gathered):
    (
        qkv_matrix,
        out_matrix,
        first_matrix,
        second_matrix,
        gain_rows,
        shift_rows,
        scale_rows,
        qv_part,
        first_bias,
    ) = gathered
    gain_float = gain_rows.astype(jnp.float32)
    shift_float = shift_rows.astype(jnp.float32)
    scale_float = scale_rows.astype(jnp.float32)
    qv_float = qv_part.astype(jnp.float32)
    images, local_rows, features = stream.shape
    normed = norm_rows(stream, gain_float[0], shift_float[0]).astype(jnp.bfloat16)
    qkv_bias = jnp.concatenate(
        [qv_float[:features], jnp.zeros((features,), jnp.float32), qv_float[features:]]
    )
    projected = (
        jnp.einsum("bsd,de->bse", normed, qkv_matrix, preferred_element_type=jnp.float32) + qkv_bias
    )
    projected = projected.astype(jnp.bfloat16).reshape(images, local_rows, 3, features)
    head_blocks = lax.all_to_all(projected, "seq", split_axis=3, concat_axis=1, tiled=True)
    attended_heads, log_totals = attention_forward(head_blocks, keep_keys)
    attended = lax.all_to_all(attended_heads, "seq", split_axis=1, concat_axis=2, tiled=True)
    branch = (
        jnp.einsum("bsd,de->bse", attended, out_matrix, preferred_element_type=jnp.float32)
        + shift_float[2]
    )
    middle = stream + scale_float[0] * branch
    normed_two = norm_rows(middle, gain_float[1], shift_float[1]).astype(jnp.bfloat16)
    hidden = jnp.einsum(
        "bsd,df->bsf", normed_two, first_matrix, preferred_element_type=jnp.float32
    ) + first_bias.astype(jnp.float32)
    activated = gelu_exact(hidden).astype(jnp.bfloat16)
    mlp_out = (
        jnp.einsum("bsf,fd->bsd", activated, second_matrix, preferred_element_type=jnp.float32)
        + shift_float[3]
    )
    remembered = (
        stream,
        normed,
        head_blocks,
        log_totals,
        attended,
        branch,
        middle,
        normed_two,
        hidden,
        activated,
        mlp_out,
    )
    return (middle + scale_float[1] * mlp_out, remembered)


def backward_layer(upstream, remembered, gathered, keep_keys):
    (
        stream,
        normed,
        head_blocks,
        log_totals,
        attended,
        branch,
        middle,
        normed_two,
        hidden,
        activated,
        mlp_out,
    ) = remembered
    (qkv_matrix, out_matrix, first_matrix, second_matrix, gain_rows, shift_rows, scale_rows, _, _) = gathered
    gain_float = gain_rows.astype(jnp.float32)
    shift_float = shift_rows.astype(jnp.float32)
    scale_float = scale_rows.astype(jnp.float32)
    images, local_rows, features = upstream.shape
    scale_two_grad = jnp.sum(upstream * mlp_out, axis=(0, 1))
    grad_mlp = (scale_float[1] * upstream).astype(jnp.bfloat16)
    second_matrix_grad = jnp.einsum(
        "bsf,bsd->fd", activated, grad_mlp, preferred_element_type=jnp.float32
    )
    mlp_bias_grad = jnp.sum(grad_mlp.astype(jnp.float32), axis=(0, 1))
    grad_act = jnp.einsum(
        "bsd,fd->bsf", grad_mlp, second_matrix, preferred_element_type=jnp.float32
    )
    _, gelu_pullback = jax.vjp(gelu_exact, hidden)
    grad_hidden = gelu_pullback(grad_act)[0].astype(jnp.bfloat16)
    first_matrix_grad = jnp.einsum(
        "bsd,bsf->df", normed_two, grad_hidden, preferred_element_type=jnp.float32
    )
    first_bias_grad = jnp.sum(grad_hidden.astype(jnp.float32), axis=(0, 1))
    grad_norm_two = jnp.einsum(
        "bsf,df->bsd", grad_hidden, first_matrix, preferred_element_type=jnp.float32
    )
    _, second_norm_pullback = jax.vjp(norm_rows, middle, gain_float[1], shift_float[1])
    grad_middle, second_gain_grad, second_shift_grad = second_norm_pullback(grad_norm_two)
    grad_middle = upstream + grad_middle
    scale_one_grad = jnp.sum(grad_middle * branch, axis=(0, 1))
    grad_branch = (scale_float[0] * grad_middle).astype(jnp.bfloat16)
    out_matrix_grad = jnp.einsum(
        "bsd,bse->de", attended, grad_branch, preferred_element_type=jnp.float32
    )
    branch_bias_grad = jnp.sum(grad_branch.astype(jnp.float32), axis=(0, 1))
    grad_attended = jnp.einsum(
        "bse,de->bsd", grad_branch, out_matrix, preferred_element_type=jnp.float32
    ).astype(jnp.bfloat16)
    grad_heads = lax.all_to_all(grad_attended, "seq", split_axis=2, concat_axis=1, tiled=True)
    grad_blocks = attention_backward(head_blocks, log_totals, grad_heads, keep_keys)
    grad_projected = lax.all_to_all(
        grad_blocks, "seq", split_axis=1, concat_axis=3, tiled=True
    ).reshape(images, local_rows, 3 * features)
    qkv_matrix_grad = jnp.einsum(
        "bsd,bse->de", normed, grad_projected, preferred_element_type=jnp.float32
    )
    column_sums = jnp.sum(grad_projected.astype(jnp.float32), axis=(0, 1))
    qv_bias_grad = jnp.concatenate([column_sums[:features], column_sums[2 * features :]])
    grad_normed = jnp.einsum(
        "bse,de->bsd", grad_projected, qkv_matrix, preferred_element_type=jnp.float32
    )
    _, first_norm_pullback = jax.vjp(norm_rows, stream, gain_float[0], shift_float[0])
    grad_stream, first_gain_grad, first_shift_grad = first_norm_pullback(grad_normed)
    grad_stream = grad_middle + grad_stream
    gradients = (
        qkv_matrix_grad,
        out_matrix_grad,
        first_matrix_grad,
        second_matrix_grad,
        jnp.stack([first_gain_grad, second_gain_grad]),
        jnp.stack([first_shift_grad, second_shift_grad, branch_bias_grad, mlp_bias_grad]),
        jnp.stack([scale_one_grad, scale_two_grad]),
        qv_bias_grad,
        first_bias_grad,
    )
    return (grad_stream, gradients)


def shards(
    images_in,
    valid,
    cotangent,
    qkv_weight,
    out_weight,
    fc1_weight,
    fc2_weight,
    gains,
    shifts,
    layer_scales,
    qv_bias,
    fc1_bias,
):
    parameters = (
        qkv_weight,
        out_weight,
        fc1_weight,
        fc2_weight,
        gains,
        shifts,
        layer_scales,
        qv_bias,
        fc1_bias,
    )
    devices = lax.axis_size(("dp", "seq"))
    keep_keys = valid > 0
    stream = images_in.astype(jnp.float32)
    remembered_layers = []
    fetched_layers = []
    for layer_index in range(LAYERS):
        gathered = fetch_layer(tuple((parameter[layer_index] for parameter in parameters)))
        stream, remembered = forward_layer(stream, keep_keys, gathered)
        remembered_layers.append(remembered)
        fetched_layers.append(gathered)
    images_out = stream.astype(jnp.bfloat16)
    local_rows = images_in.shape[1]
    row_valid = lax.dynamic_slice_in_dim(valid, lax.axis_index("seq") * local_rows, local_rows, 1)
    upstream = cotangent.astype(jnp.float32) * row_valid.astype(jnp.float32)[:, :, None]
    collected = [None] * LAYERS
    for layer_index in range(LAYERS - 1, -1, -1):
        gathered = fetched_layers[layer_index]
        upstream, gradients = backward_layer(
            upstream, remembered_layers[layer_index], gathered, keep_keys
        )
        collected[layer_index] = scatter_layer(gradients, devices)
    stacked = tuple(
        (
            jnp.stack([collected[layer_index][member] for layer_index in range(LAYERS)])
            for member in range(9)
        )
    )
    return (images_out, upstream.astype(jnp.bfloat16)) + tuple(stacked)


F32=jnp.float32; BF=jnp.bfloat16
NN=(((1,),(0,)),((),())); NT=(((1,),(1,)),((),())); TN=(((0,),(0,)),((),()))
dd=functools.partial(lax.dot_general,preferred_element_type=F32)
LIMIT=pltpu.CompilerParams(vmem_limit_bytes=60<<20)

def normalize(v):
    c=v-jnp.mean(v,axis=-1,keepdims=True)
    r=lax.rsqrt(jnp.mean(c*c,axis=-1,keepdims=True)+epsilon)
    return c*r,r

def const(*shape): return pl.BlockSpec(shape,lambda *_: (0,)*len(shape))

def grid_with(grid,in_specs,out_specs,scratch):
    return pltpu.PrefetchScalarGridSpec(num_scalar_prefetch=1,grid=grid,in_specs=in_specs,out_specs=out_specs,scratch_shapes=scratch)

def by_distance(idx,src,outs,at=None):
    g=src.shape[1]//len(outs)
    for k,out in enumerate(outs):
        piece=src[:,pl.ds(pl.multiple_of(jnp.bitwise_xor(idx[4],k)*g,128),g)]
        if at is None: out[...]=piece
        else: out[at]=piece

def in_order(idx,pieces,dst):
    g=dst.shape[1]//len(pieces)
    for k,piece in enumerate(pieces):
        dst[:,pl.ds(pl.multiple_of(jnp.bitwise_xor(idx[4],k)*g,128),g)]=piece

def places(idx,color):
    for dc in range(2):
        for outer in range(2):
            for inner in range(2):
                dy,dx=(outer,inner) if color==0 else (inner,outer)
                c=jnp.bitwise_xor(idx[0],dc); y=jnp.bitwise_xor(idx[2],dy); x=jnp.bitwise_xor(idx[3],dx)
                yield dc*2+outer,inner,(c*2+y)*2+x

def lay_units(idx,color,refs,dst):
    for ref,inner,cyx in places(idx,color):
        for dz in range(4):
            row=(jnp.bitwise_xor(idx[1],dz)*8+cyx)*32
            dst[pl.ds(pl.multiple_of(row,32),32),:]=refs[ref][inner,dz]

def lay_rows(idx,color,refs,dst):
    for ref,inner,cyx in places(idx,color):
        dst[pl.ds(pl.multiple_of(cyx*128,128),128),:]=refs[ref][inner,0]

def qkv_kernel(idx,stream_ref,vec_ref,w_ref,normed_ref,*rest):
    outs,scr=rest[:-1],rest[-1]
    p=pl.program_id(0)
    @pl.when(p==0)
    def _():
        x,_=normalize(stream_ref[...])
        normed_ref[...]=(x*vec_ref[0:1,:]+vec_ref[2:3,:]).astype(BF)
    width=w_ref.shape[-1]
    y=dd(normed_ref[...],w_ref[...].reshape(-1,width),NN)
    b=jnp.where(p==0,vec_ref[8:9,:],jnp.where(p==2,vec_ref[9:10,:],0.0))
    scr[...]=(y+b).astype(BF)
    by_distance(idx,scr,outs,0)

def qkv_forward(idx,stream,vec,wa,groups):
    T,D=stream.shape
    n=wa.shape[0]
    S=jax.ShapeDtypeStruct
    res=pl.pallas_call(qkv_kernel,
        out_shape=(S((T,D),BF),)+(S((3,T,D//groups),BF),)*groups,
        grid_spec=grid_with((3,),[const(T,D),const(*vec.shape),pl.BlockSpec((n,4,8,D),lambda p,i:(0,p,0,0))],
            (const(T,D),)+(pl.BlockSpec((1,T,D//groups),lambda p,i:(p,0,0)),)*groups,[pltpu.VMEM((T,D),BF)]),
        compiler_params=LIMIT,name="qkv_forward")(idx,stream,vec,wa)
    return res[0],res[1:]

def gelu_pair(v):
    phi=0.5+0.5*lax.erf(v*math.sqrt(0.5))
    return v*phi, phi+v*(jnp.exp(-0.5*v*v)*(1/math.sqrt(2*math.pi)))

def mlp_kernel(idx,a0,a1,a2,a3,stream_ref,vec_ref,wo_ref,*refs):
    w1,w2=refs[:4],refs[4:8]
    branch_ref,middle_ref,n2_ref,act_ref,gp_ref,mlp_ref,next_ref,att_ref,acc,w1_s,w2_s=refs[8:]
    f=pl.program_id(0); D=stream_ref.shape[1]
    @pl.when(f==0)
    def _():
        in_order(idx,[r[...] for r in (a0,a1,a2,a3)],att_ref)
        branch=dd(att_ref[...],wo_ref[...].reshape(D,D),NN)+vec_ref[4:5,:]
        branch_ref[...]=branch
        middle=stream_ref[...]+vec_ref[6:7,:]*branch
        middle_ref[...]=middle
        x,_=normalize(middle)
        n2_ref[...]=(x*vec_ref[1:2,:]+vec_ref[3:4,:]).astype(BF)
        acc[...]=jnp.zeros_like(acc)
    lay_units(idx,0,w1,w1_s)
    lay_rows(idx,1,w2,w2_s)
    hidden=dd(n2_ref[...],w1_s[...],NN)+vec_ref[pl.ds(10+f,1),:]
    a,gp=gelu_pair(hidden)
    a=a.astype(BF)
    act_ref[...]=a; gp_ref[...]=gp.astype(BF)
    acc[...]+=dd(a,w2_s[...],NN)
    @pl.when(f==pl.num_programs(0)-1)
    def _():
        m=acc[...]+vec_ref[5:6,:]
        mlp_ref[...]=m
        next_ref[...]=middle_ref[...]+vec_ref[7:8,:]*m

def block_specs(nb,D):
    at=lambda f: jnp.minimum(f,nb-1)
    return [pl.BlockSpec((2,4,32,D),lambda f,i:(0,0,at(f),0))]*4+[pl.BlockSpec((2,1,128,D),lambda f,i:(0,jnp.bitwise_xor(at(f),i[1]),0,0))]*4

def mlp_forward(idx,att,stream,vec,wa,w1,w2):
    T,D=stream.shape; n=wa.shape[0]; nb=4
    S=jax.ShapeDtypeStruct
    hid=pl.BlockSpec((T,D),lambda f,i:(0,f))
    return pl.pallas_call(mlp_kernel,
        out_shape=(S((T,D),F32),S((T,D),F32),S((T,D),BF),S((T,nb*D),BF),S((T,nb*D),BF),S((T,D),F32),S((T,D),F32),S((T,D),BF)),
        grid_spec=grid_with((nb,),[const(T,D//4)]*4+[const(T,D),const(*vec.shape),
            pl.BlockSpec((n,4,8,D),lambda f,i:(0,3,0,0)),
            *block_specs(nb,D)],
            (const(T,D),const(T,D),const(T,D),hid,hid,const(T,D),const(T,D),const(T,D)),[pltpu.VMEM((T,D),F32)]+[pltpu.VMEM((D,D),BF)]*2),
        compiler_params=LIMIT,name="mlp_forward")(idx,*att,stream,vec,wa,*w1,*w2)

def norm_back(v,u,gain):
    x,r=normalize(v)
    w=u*gain
    dv=r*(w-jnp.mean(w,axis=-1,keepdims=True)-x*jnp.mean(w*x,axis=-1,keepdims=True))
    return dv,jnp.sum(u*x,axis=0,keepdims=True),jnp.sum(u,axis=0,keepdims=True)

def mlp_back_kernel(idx,up_ref,mlp_ref,branch_ref,middle_ref,gp_ref,vec_ref,wo_ref,*refs):
    w1,w2=refs[:4],refs[4:8]
    dall_ref,dmid_ref,d0,d1,d2,d3,sums_ref,acc,dm_s,w1_s,w2_s=refs[8:]
    f=pl.program_id(0); D=up_ref.shape[1]
    nb=pl.num_programs(0)-2
    @pl.when(f==0)
    def _():
        u=up_ref[...]
        sums_ref[...]=jnp.zeros_like(sums_ref)
        sums_ref[7:8,:]=jnp.sum(u*mlp_ref[...],axis=0,keepdims=True)
        dm=(vec_ref[7:8,:]*u).astype(BF)
        dm_s[...]=dm
        sums_ref[5:6,:]=jnp.sum(dm.astype(F32),axis=0,keepdims=True)
        acc[...]=jnp.zeros_like(acc)
    @pl.when(f<nb)
    def _():
        lay_units(idx,0,w1,w1_s)
        lay_rows(idx,1,w2,w2_s)
        da=dd(dm_s[...],w2_s[...],NT)
        dh=(da*gp_ref[...].astype(F32)).astype(BF)
        dall_ref[...]=dh
        sums_ref[pl.ds(10+f,1),:]=jnp.sum(dh.astype(F32),axis=0,keepdims=True)
        acc[...]+=dd(dh,w1_s[...],NT)
    @pl.when(f==nb)
    def _():
        dall_ref[...]=dm_s[...]
    @pl.when(f==nb+1)
    def _():
        dv,dg,ds=norm_back(middle_ref[...],acc[...],vec_ref[1:2,:])
        sums_ref[1:2,:]=dg; sums_ref[3:4,:]=ds
        dmid=up_ref[...]+dv
        dmid_ref[...]=dmid
        sums_ref[6:7,:]=jnp.sum(dmid*branch_ref[...],axis=0,keepdims=True)
        db=(vec_ref[6:7,:]*dmid).astype(BF)
        dall_ref[...]=db
        sums_ref[4:5,:]=jnp.sum(db.astype(F32),axis=0,keepdims=True)
        dm_s[...]=dd(db,wo_ref[...].reshape(D,D),NT).astype(BF)
        by_distance(idx,dm_s,(d0,d1,d2,d3))

def mlp_backward(idx,up,mlp,branch,middle,gp,vec,wa,w1,w2):
    T,D=up.shape; n=wa.shape[0]; nb=4
    S=jax.ShapeDtypeStruct
    last=lambda f: jnp.minimum(f,nb-1)
    res=pl.pallas_call(mlp_back_kernel,
        out_shape=(S((T,(nb+2)*D),BF),S((T,D),F32))+(S((T,D//4),BF),)*4+(S((16,D),F32),),
        grid_spec=grid_with((nb+2,),[const(T,D)]*4+[pl.BlockSpec((T,D),lambda f,i:(0,last(f))),const(*vec.shape),
            pl.BlockSpec((n,4,8,D),lambda f,i:(0,3,0,0)),
            *block_specs(nb,D)],
            (pl.BlockSpec((T,D),lambda f,i:(0,f)),const(T,D))+(const(T,D//4),)*4+(const(16,D),),
            [pltpu.VMEM((T,D),F32),pltpu.VMEM((T,D),BF)]+[pltpu.VMEM((D,D),BF)]*2),
        compiler_params=LIMIT,name="mlp_backward")(idx,up,mlp,branch,middle,gp,vec,wa,*w1,*w2)
    return res[0],res[1],res[2:6],res[6]

def qkv_back_kernel(idx,p0,p1,p2,p3,stream_ref,dmid_ref,vec_ref,w_ref,sums_in,up_ref,dproj_ref,sums_ref,acc):
    p=pl.program_id(0); D=stream_ref.shape[1]
    @pl.when(p==0)
    def _():
        acc[...]=jnp.zeros_like(acc)
        sums_ref[...]=sums_in[...]
    in_order(idx,[r[0] for r in (p0,p1,p2,p3)],dproj_ref)
    d=dproj_ref[...]
    acc[...]+=dd(d,w_ref[...].reshape(D,D),NT)
    col=jnp.sum(d.astype(F32),axis=0,keepdims=True)
    @pl.when(p==0)
    def _(): sums_ref[8:9,:]=col
    @pl.when(p==2)
    def _():
        sums_ref[9:10,:]=col
        dv,dg,ds=norm_back(stream_ref[...],acc[...],vec_ref[0:1,:])
        sums_ref[0:1,:]=dg; sums_ref[2:3,:]=ds
        up_ref[...]=dmid_ref[...]+dv

def qkv_backward(idx,dp,stream,dmid,vec,wa,sums):
    T,D=stream.shape; n=wa.shape[0]
    S=jax.ShapeDtypeStruct
    return pl.pallas_call(qkv_back_kernel,
        out_shape=(S((T,D),F32),S((T,3*D),BF),S((16,D),F32)),
        grid_spec=grid_with((3,),[pl.BlockSpec((1,T,D//4),lambda p,i:(p,0,0))]*4+[const(T,D),const(T,D),const(*vec.shape),
            pl.BlockSpec((n,4,8,D),lambda p,i:(0,p,0,0)),const(16,D)],
            (const(T,D),pl.BlockSpec((T,D),lambda p,i:(0,p)),const(16,D)),[pltpu.VMEM((T,D),F32)]),
        compiler_params=LIMIT,name="qkv_backward")(idx,*dp,stream,dmid,vec,wa,sums)


def attn_fwd_kernel(*refs, chunks):
    qkv=refs[:chunks]; valid_ref=refs[chunks]; outs=refs[chunks+1:2*chunks+1]; lse_ref=refs[2*chunks+1]; q_s,k_s,v_s=refs[2*chunks+2:]
    i=pl.program_id(0)
    rows,width=qkv[0].shape[1:]
    heads=width//HD
    @pl.when(i==0)
    def _():
        for j in range(chunks):
            q_s[j]=qkv[j][0]*jnp.bfloat16(HD**-0.5)
            k_s[j*rows:(j+1)*rows,:]=qkv[j][1]
            v_s[j*rows:(j+1)*rows,:]=qkv[j][2]
    q=q_s[i]
    lane=lax.broadcasted_iota(jnp.int32,(1,width),1)//HD
    col=lax.broadcasted_iota(jnp.int32,(1,128),1)
    keep=valid_ref[...]>0
    acc=jnp.zeros((rows,width),jnp.float32)
    stats=jnp.zeros((rows,128),jnp.float32)
    for h in range(heads):
        qh=jnp.where(lane==h,q,jnp.zeros_like(q))
        s=lax.dot_general(qh,k_s[...],(((1,),(1,)),((),())),preferred_element_type=jnp.float32)
        s=jnp.where(keep,s,masked_value)
        m=jnp.max(s,axis=1,keepdims=True)
        e=jnp.exp(s-m)
        t=jnp.sum(e,axis=1,keepdims=True)
        o=lax.dot_general(e.astype(jnp.bfloat16),v_s[...],(((1,),(0,)),((),())),preferred_element_type=jnp.float32)
        acc=jnp.where(lane==h,o/t,acc)
        stats=jnp.where(col==h,m+jnp.log(t),stats)
    acc=acc.astype(jnp.bfloat16)
    for j in range(chunks):
        @pl.when(i==j)
        def _(j=j): outs[j][...]=acc
    lse_ref[0]=stats.T[0:8,:]

def attn_fwd(qkv,valid):
    chunks=len(qkv); _,rows,width=qkv[0].shape
    keys=rows*chunks
    full=lambda *s: pl.BlockSpec(s,lambda i:(0,)*len(s))
    S=jax.ShapeDtypeStruct
    res=pl.pallas_call(
        functools.partial(attn_fwd_kernel,chunks=chunks),
        grid=(chunks,),
        out_shape=(S((rows,width),jnp.bfloat16),)*chunks+(S((chunks,8,rows),jnp.float32),),
        in_specs=[full(3,rows,width)]*chunks+[full(1,keys)],
        out_specs=(full(rows,width),)*chunks+(pl.BlockSpec((1,8,rows),lambda i:(i,0,0)),),
        scratch_shapes=[pltpu.VMEM((chunks,rows,width),jnp.bfloat16)]+[pltpu.VMEM((keys,width),jnp.bfloat16)]*2,
        compiler_params=pltpu.CompilerParams(vmem_limit_bytes=60<<20),
        name="attention_forward",
    )(*qkv,valid)
    return res[:chunks],res[chunks]

def attn_bwd_kernel(*refs, chunks):
    qkv=refs[:chunks]; o=refs[chunks:2*chunks]; g_in=refs[2*chunks:3*chunks]
    valid_ref,lse_ref=refs[3*chunks:3*chunks+2]
    outs=refs[3*chunks+2:4*chunks+2]
    q_s,g_s,k_s,v_s,dq_s,lse_s,dl_s=refs[4*chunks+2:]
    j=pl.program_id(0)
    rows,width=qkv[0].shape[1:]
    heads=width//HD
    dd=functools.partial(lax.dot_general,preferred_element_type=jnp.float32)
    lane=lax.broadcasted_iota(jnp.int32,(1,width),1)//HD
    @pl.when(j==0)
    def _():
        hm=(lax.broadcasted_iota(jnp.int32,(8,width),1)//HD==lax.broadcasted_iota(jnp.int32,(8,width),0)).astype(jnp.float32)
        for c in range(chunks):
            sl=slice(c*rows,(c+1)*rows)
            q_s[sl,:]=qkv[c][0]*jnp.bfloat16(HD**-0.5)
            k_s[c]=qkv[c][1]; v_s[c]=qkv[c][2]
            g=g_in[c][...]
            g_s[sl,:]=g
            prod=g.astype(jnp.float32)*o[c][...].astype(jnp.float32)
            dl_s[:,sl]=lax.dot_general(hm,prod,(((1,),(1,)),((),())),precision=lax.Precision.HIGHEST,preferred_element_type=jnp.float32)
            lse_s[:,sl]=lse_ref[c]
        dq_s[...]=jnp.zeros_like(dq_s)
    k=k_s[j]; v=v_s[j]
    keep=valid_ref[0]>0
    dk=jnp.zeros((rows,width),jnp.float32); dv=jnp.zeros((rows,width),jnp.float32)
    q=q_s[...]; g=g_s[...]
    zero=jnp.zeros_like(k)
    for h in range(heads):
        sel=lane==h
        kh=jnp.where(sel,k,zero); vh=jnp.where(sel,v,zero)
        s=dd(kh,q,(((1,),(1,)),((),())))
        s=jnp.where(keep,s,masked_value)
        p=jnp.exp(s-lse_s[h:h+1,:])
        dp=dd(vh,g,(((1,),(1,)),((),())))
        ds=(p*(dp-dl_s[h:h+1,:])).astype(jnp.bfloat16)
        dv=jnp.where(sel,dd(p.astype(jnp.bfloat16),g,(((1,),(0,)),((),()))),dv)
        dk=jnp.where(sel,dd(ds,q,(((1,),(0,)),((),()))),dk)
        dq_s[...]+=dd(ds,kh,(((0,),(0,)),((),())))
    dk=dk.astype(jnp.bfloat16); dv=dv.astype(jnp.bfloat16)
    for c in range(chunks):
        @pl.when(j==c)
        def _(c=c):
            outs[c][1]=dk
            outs[c][2]=dv
    @pl.when(j==chunks-1)
    def _():
        for c in range(chunks):
            outs[c][0]=(dq_s[c*rows:(c+1)*rows,:]*HD**-0.5).astype(jnp.bfloat16)

def attn_bwd(qkv,valid_col,o,g,lse):
    chunks=len(qkv); _,rows,width=qkv[0].shape
    keys=rows*chunks
    full=lambda *s: pl.BlockSpec(s,lambda j:(0,)*len(s))
    return pl.pallas_call(
        functools.partial(attn_bwd_kernel,chunks=chunks),
        grid=(chunks,),
        out_shape=(jax.ShapeDtypeStruct((3,rows,width),jnp.bfloat16),)*chunks,
        in_specs=[full(3,rows,width)]*chunks+[full(rows,width)]*(2*chunks)+[pl.BlockSpec((1,rows,1),lambda j:(j,0,0)),full(chunks,8,rows)],
        out_specs=(full(3,rows,width),)*chunks,
        scratch_shapes=[pltpu.VMEM((keys,width),jnp.bfloat16)]*2+[pltpu.VMEM((chunks,rows,width),jnp.bfloat16)]*2+[pltpu.VMEM((keys,width),jnp.float32)]+[pltpu.VMEM((8,keys),jnp.float32)]*2,
        compiler_params=pltpu.CompilerParams(vmem_limit_bytes=60<<20),
        name="attention_backward",
    )(*qkv,*o,*g,valid_col,lse)


def spread(color,idx,keep_ref,send_ref,write):
    my,mx=idx[2],idx[3]
    for d in range(2):
        for sent,ref in ((0,keep_ref),(1,send_ref)):
            y=jnp.bitwise_xor(my,d if color==0 else sent)
            x=jnp.bitwise_xor(mx,sent if color==0 else d)
            write(ref,d,y*2+x)

def write_units(color,idx,at,scr,keep_ref,send_ref):
    def write(ref,d,yx):
        for dz in range(4):
            row=pl.multiple_of(jnp.bitwise_xor(idx[1],dz)*128+yx*32,32)
            ref[d,dz,at:at+32,:]=scr[pl.ds(row,32),:]
    spread(color,idx,keep_ref,send_ref,write)

def write_vectors(color,idx,vec_ref,keep_ref,send_ref):
    def write(ref,d,yx):
        for dz in range(4):
            ref[d,dz,64:72,:]=vec_ref[(jnp.bitwise_xor(idx[1],dz)*2+idx[0])*4+yx]
    spread(color,idx,keep_ref,send_ref,write)

def lhs_columns(idx,ref):
    return jnp.concatenate([ref[:,pl.ds(pl.multiple_of((2*z+idx[0])*128,128),128)] for z in range(4)],axis=1)

def pair_product(a,b,x,y):
    return (dd(a,b,TN)+dd(x,y,TN)).astype(BF)

def second_grad_kernel(idx,a_ref,x_ref,b_ref,y_ref,keep_ref,send_ref,scr):
    scr[...]=pair_product(a_ref[...],b_ref[...],x_ref[...],y_ref[...])
    def write(ref,d,yx):
        ref[d,0]=scr[pl.ds(pl.multiple_of(yx*128,128),128),:]
    spread(0,idx,keep_ref,send_ref,write)

def second_grad(idx,act,act_o,dall,dall_o):
    T=act.shape[0]; D=1024
    S=jax.ShapeDtypeStruct((2,4,128,D),BF)
    xs=pl.BlockSpec((T,512),lambda s,i:(0,2*s+i[0])); ys=pl.BlockSpec((T,D),lambda s,i:(0,4))
    out=pl.BlockSpec((2,1,128,D),lambda s,i:(0,jnp.bitwise_xor(s,i[1]),0,0))
    return pl.pallas_call(second_grad_kernel,out_shape=(S,S),
        grid_spec=pltpu.PrefetchScalarGridSpec(num_scalar_prefetch=1,grid=(4,),in_specs=[xs,xs,ys,ys],out_specs=(out,out),
            scratch_shapes=[pltpu.VMEM((512,D),BF)]),
        compiler_params=LIMIT,name="second_grad")(idx,act,act_o,dall,dall_o)

def first_grad_kernel(idx,a_ref,x_ref,b_ref,y_ref,keep_ref,send_ref,scr):
    scr[...]=pair_product(lhs_columns(idx,a_ref),b_ref[...],lhs_columns(idx,x_ref),y_ref[...])
    s=pl.program_id(0)
    for u in range(4):
        @pl.when(s==u)
        def _(u=u): write_units(1,idx,32*u,scr,keep_ref,send_ref)

def first_grad(idx,n2,n2_o,dall,dall_o):
    T,D=n2.shape
    S=jax.ShapeDtypeStruct((2,4,128,D),BF)
    xs=pl.BlockSpec((T,D),lambda s,i:(0,0)); ys=pl.BlockSpec((T,D),lambda s,i:(0,s))
    out=pl.BlockSpec((2,4,128,D),lambda s,i:(0,0,0,0))
    return pl.pallas_call(first_grad_kernel,out_shape=(S,S),
        grid_spec=pltpu.PrefetchScalarGridSpec(num_scalar_prefetch=1,grid=(4,),in_specs=[xs,xs,ys,ys],out_specs=(out,out),
            scratch_shapes=[pltpu.VMEM((512,D),BF)]),
        compiler_params=LIMIT,name="first_grad")(idx,n2,n2_o,dall,dall_o)

def attention_grad_kernel(idx,att_ref,att_o,norm_ref,norm_o,db_ref,db_o,dp_ref,dp_o,vec_ref,keep_a,send_a,keep_b,send_b,scr):
    s=pl.program_id(0)
    @pl.when(s==0)
    def _():
        scr[...]=pair_product(lhs_columns(idx,att_ref),db_ref[...],lhs_columns(idx,att_o),db_o[...])
        write_units(0,idx,0,scr,keep_a,send_a)
        write_vectors(0,idx,vec_ref,keep_a,send_a)
    @pl.when(s>0)
    def _():
        scr[...]=pair_product(lhs_columns(idx,norm_ref),dp_ref[...],lhs_columns(idx,norm_o),dp_o[...])
    @pl.when(s==1)
    def _(): write_units(0,idx,32,scr,keep_a,send_a)
    for u in (0,1):
        @pl.when(s==2+u)
        def _(u=u): write_units(1,idx,32*u,scr,keep_b,send_b)

def attention_grad(idx,att,att_o,normed,normed_o,dall,dall_o,dp,dp_o,vec):
    T,D=normed.shape
    A=jax.ShapeDtypeStruct((2,4,72,D),BF); B=jax.ShapeDtypeStruct((2,4,64,D),BF)
    full=lambda a: pl.BlockSpec(a.shape,lambda s,i:(0,)*len(a.shape))
    db=pl.BlockSpec((T,D),lambda s,i:(0,5)); dps=pl.BlockSpec((T,D),lambda s,i:(0,jnp.maximum(s-1,0)))
    return pl.pallas_call(attention_grad_kernel,out_shape=(A,A,B,B),
        grid_spec=pltpu.PrefetchScalarGridSpec(num_scalar_prefetch=1,grid=(4,),
            in_specs=[full(att),full(att),full(normed),full(normed),db,db,dps,dps,full(vec)],out_specs=(full(A),full(A),full(B),full(B)),
            scratch_shapes=[pltpu.VMEM((512,D),BF)]),
        compiler_params=LIMIT,name="attention_grad")(idx,att,att_o,normed,normed_o,dall,dall_o,dp,dp_o,vec)

def is_fast(mesh):
    return mesh.shape["dp"]==8 and mesh.shape["seq"]==4

def swap(v,axis,step):
    return lax.ppermute(v,axis,[(i,i^step) for i in range(lax.axis_size(axis))])

def exchange(pieces):
    return tuple(pieces[:1])+tuple(swap(pieces[k],"seq",k) for k in range(1,4))

def add(a,b):
    return (a.astype(F32)+b.astype(F32)).astype(BF)

def across_first(keep_a,send_a,keep_b,send_b):
    got_a=swap(send_a,"seq",1); got_b=swap(send_b,"seq",2)
    return (add(keep_a[0],got_a[0]),add(keep_a[1],got_a[1]),add(keep_b[0],got_b[0]),add(keep_b[1],got_b[1]))

def across_second(sums):
    stay_a,next_a,stay_b,next_b=sums
    got_a=swap(next_a,"seq",2); got_b=swap(next_b,"seq",1)
    rows=lambda v: v.reshape(4,-1,v.shape[-1])
    return jnp.concatenate([rows(add(stay_a,got_a)),rows(add(stay_b,got_b))],axis=1)

def across_third(whole):
    got=[swap(whole[step],"dp",2*step) for step in range(1,4)]
    return sum((g.astype(F32) for g in got),whole[0].astype(F32))

def collect(parts):
    return across_third(across_second(across_first(*parts)))

def gather_pair(a,b):
    whole=jnp.concatenate([a,b],axis=0)
    got=[whole]+[swap(whole,"dp",2*step) for step in range(1,4)]
    cut=a.shape[0]
    za=jnp.stack([g[:cut] for g in got]); zb=jnp.stack([g[cut:] for g in got])
    xa=jnp.stack([za,swap(za,"seq",1)]); yb=jnp.stack([zb,swap(zb,"seq",2)])
    ya=swap(xa,"seq",2); xb=swap(yb,"seq",1)
    core=lambda v: swap(v,"dp",1)
    return (xa,ya,core(xa),core(ya)),(yb,xb,core(yb),core(xb))

def fast_body(images_in,valid,cotangent,qkv_weight,out_weight,fc1_weight,fc2_weight,gains,shifts,layer_scales,qv_bias,fc1_bias):
    layers=qkv_weight.shape[0]
    rows,D=out_weight.shape[1:]
    T=images_in.shape[1]
    n=lax.axis_size(("dp","seq")); G=lax.axis_size("seq")
    dp=lax.axis_index("dp"); seq=lax.axis_index("seq")
    idx=jnp.stack([dp%2,dp//2,seq//2,seq%2,seq]).astype(jnp.int32)
    units=lambda m: m.reshape(rows,-1,D).transpose(1,0,2).reshape(-1,D)
    vectors=jnp.concatenate([v.reshape(layers,-1) for v in (gains,shifts,layer_scales,qv_bias,fc1_bias)],axis=1)
    size=vectors.shape[1]
    extra=jnp.zeros((8,D),BF).at[:layers,:size].set(vectors)
    gather=lambda *pieces: lax.all_gather(jnp.concatenate(pieces,axis=0),("dp","seq"),axis=0,tiled=False).reshape(n,-1,8,D)
    wa=[gather(units(qkv_weight[l]),out_weight[l],*([extra] if l==0 else [])) for l in range(layers)]
    w1=[];w2=[]
    for l in range(layers):
        one,two=gather_pair(units(fc1_weight[l]),fc2_weight[l])
        w1.append(one); w2.append(two)
    flat=wa[0][:,4*rows//8,:layers,:size].astype(F32)
    part=8*rows
    first=flat[:,:,:part].reshape(n,layers,8,rows).transpose(1,2,0,3).reshape(layers,8,D)
    second=flat[:,:,part:part+2*rows].transpose(1,0,2).reshape(layers,2,D)
    third=flat[:,:,part+2*rows:].transpose(1,0,2).reshape(layers,4,D)
    vecs=jnp.concatenate([first,second,third,jnp.zeros((layers,2,D),F32)],axis=1)
    tokens=valid.reshape(G,T)
    tokens=jnp.stack([lax.dynamic_index_in_dim(tokens,seq^k,0,False) for k in range(G)])
    line=tokens.reshape(1,G*T); column=tokens.reshape(G,T,1)
    stream=images_in[0].astype(F32)
    keep=[]
    for l in range(layers):
        normed,proj=qkv_forward(idx,stream,vecs[l],wa[l],G)
        heads=exchange(proj)
        out,lse=attn_fwd(heads,line)
        att=exchange(out)
        branch,middle,n2,act,gp,mlp,after,att=mlp_forward(idx,att,stream,vecs[l],wa[l],w1[l],w2[l])
        others=[swap(v,"dp",1) for v in (normed,att,n2,act)]
        keep.append((stream,normed,heads,out,lse,att,branch,middle,n2,act,gp,mlp,others))
        stream=after
    images_out=stream.astype(BF)[None]
    up=cotangent[0].astype(F32)*tokens[0].astype(F32)[:,None]
    done=[None]*layers
    def by_device(v):
        size=rows*8
        flat=jnp.concatenate([v[:8].reshape(8,n,rows).transpose(1,0,2).reshape(n,size),v[8:10].reshape(n,2*rows),v[10:14].reshape(n,4*rows)],axis=1)
        return jnp.pad(flat.reshape(n,1,-1),((0,0),(0,7),(0,D-flat.shape[1])))
    for l in range(layers-1,-1,-1):
        stream,normed,heads,out,lse,att,branch,middle,n2,act,gp,mlp,(normed_o,att_o,n2_o,act_o)=keep[l]
        dall,dmid,datt,sums=mlp_backward(idx,up,mlp,branch,middle,gp,vecs[l],wa[l],w1[l],w2[l])
        dheads=exchange(datt)
        dall_o=swap(dall,"dp",1)
        sg=second_grad(idx,act,act_o,dall,dall_o)
        fg=first_grad(idx,n2,n2_o,dall,dall_o)
        mlp_total=collect((*sg,*fg))
        dqkv=attn_bwd(heads,column,out,dheads,lse)
        dproj=exchange(dqkv)
        up,dproj,sums=qkv_backward(idx,dproj,stream,dmid,vecs[l],wa[l],sums)
        dproj_o=swap(dproj,"dp",1)
        both=by_device(sums+swap(sums,"dp",1)).astype(BF)
        ag=attention_grad(idx,att,att_o,normed,normed_o,dall,dall_o,dproj,dproj_o,both)
        att_total=collect(ag)
        done[l]=(mlp_total,att_total)
    flat=jnp.stack([done[l][1][2*rows] for l in range(layers)])
    part=rows*8
    small=flat[:,:part].reshape(layers,8,rows)
    qv=flat[:,part:part+2*rows]; bias=flat[:,part+2*rows:part+6*rows]
    wide=lambda v: v.reshape(-1,rows,D).transpose(1,0,2).reshape(rows,-1)
    join=lambda f: jnp.stack([f(*done[l]) for l in range(layers)])
    gq=join(lambda m,a: wide(jnp.concatenate([a[rows:2*rows],a[2*rows+8:]],axis=0)))
    go=join(lambda m,a: a[:rows])
    g1=join(lambda m,a: wide(m[4*rows:8*rows]))
    g2=join(lambda m,a: m[:4*rows])
    return (images_out,up.astype(BF)[None],gq,go,g1,g2,small[:,0:2],small[:,2:6],small[:,6:8],qv,bias)


def solution(mesh):
    in_specs = (
        P("dp", "seq", None),
        P("dp", None),
        P("dp", "seq", None),
        P(None, ("dp", "seq"), None),
        P(None, ("dp", "seq"), None),
        P(None, ("dp", "seq"), None),
        P(None, ("dp", "seq"), None),
        P(None, None, ("dp", "seq")),
        P(None, None, ("dp", "seq")),
        P(None, None, ("dp", "seq")),
        P(None, ("dp", "seq")),
        P(None, ("dp", "seq")),
    )
    out_specs = (
        P("dp", "seq", None),
        P("dp", "seq", None),
        P(None, ("dp", "seq"), None),
        P(None, ("dp", "seq"), None),
        P(None, ("dp", "seq"), None),
        P(None, ("dp", "seq"), None),
        P(None, None, ("dp", "seq")),
        P(None, None, ("dp", "seq")),
        P(None, None, ("dp", "seq")),
        P(None, ("dp", "seq")),
        P(None, ("dp", "seq")),
    )
    if not is_fast(mesh):
        return jax.shard_map(shards, mesh=mesh, in_specs=in_specs, out_specs=out_specs, check_vma=False)
    return jax.shard_map(fast_body, mesh=mesh, in_specs=in_specs, out_specs=out_specs, check_vma=False)
```
